256 devices in a mesh: tile: 64 (over z, y_lo, x), chan: 4 (over y_hi, core).
Axes of the slice: x: 4, y: 4 (y_hi: 2, y_lo: 2; y = y_hi * 2 + y_lo), z: 8, core: 2. Of those that a mesh axis runs over, the one named last changes fastest.
Arguments:
- latent: bfloat16 [2, 16, 14400], P(None, 'chan', 'tile'), may hold values from -6 to 6
- latent_cache: bfloat16 [2, 16, 14400], P(None, 'chan', 'tile'), may hold values from -6 to 6
- weight_in: bfloat16 [3, 3, 3, 384, 16], P(None, None, None, 'chan'), may hold values from -0.3125 to 0.3125
- bias_in: float32 [384], P('chan'), may hold values from -3 to 3
- cache_a: bfloat16 [2, 384, 14400], P(None, 'chan', 'tile'), may hold values from -6 to 6
- gain_a: float32 [384], P('chan'), may hold values from 0.1 to 1.9
- weight_a: bfloat16 [3, 3, 3, 384, 384], P(None, None, None, 'chan'), may hold values from -0.0625 to 0.0625
- bias_a: float32 [384], P('chan'), may hold values from -3 to 3
- cache_b: bfloat16 [2, 384, 14400], P(None, 'chan', 'tile'), may hold values from -6 to 6
- gain_b: float32 [384], P('chan'), may hold values from 0.1 to 1.9
- weight_b: bfloat16 [3, 3, 3, 384, 384], P(None, None, None, 'chan'), may hold values from -0.0625 to 0.0625
- bias_b: float32 [384], P('chan'), may hold values from -3 to 3
- weight_up: bfloat16 [3, 3, 192, 384], P(None, None, 'chan'), may hold values from -0.109375 to 0.109375
- bias_up: float32 [192], P('chan'), may hold values from -3 to 3
Outputs:
- upsampled: bfloat16 [2, 192, 57600], P(None, 'chan', 'tile')
The draws below stay inside these ranges and needn't reach their ends.
All inputs are finite; a program needn't handle non-finite values.
Results may differ from the reference program's by a relative error of at most 0.011.
Values may be sent and summed in bfloat16 or wider, within the bound.
A program may use at most 64 MiB of HBM per device.

```python
import jax
import jax.numpy as jnp
from jax import lax

C = 384
CU = 192
Z = 16
W = 160
H = 90
F = 2


def steps_of(key, extent, shards, smallest, high):
    factor_of = 1.0
    for axis_at, parts in shards:
        steps = jax.random.uniform(jax.random.fold_in(jax.random.fold_in(key, 6), axis_at), (parts,), jnp.float32, smallest / len(shards), high / len(shards))
        factor_of = factor_of * jnp.repeat(jnp.exp(steps), extent[axis_at] // parts).reshape((-1,) + (1,) * (len(extent) - 1 - axis_at))
    return factor_of


def centred(key, shape, width, limit, shards=(), dtype=jnp.bfloat16):
    entries = jax.random.normal(key, shape, jnp.float32) * width
    if len(shards) > 0:
        entries = steps_of(key, shape, shards, -0.22, 0.18) * entries
    return jnp.clip(entries, min=-limit, max=limit).astype(dtype)


def setup_inputs(seed: int = 0) -> dict:
    arg_keys = jax.random.split(jax.random.key(seed), 15)
    latent = centred(arg_keys[0], (F, Z, H * W), 1.0, 6.0, ((1, 4), (2, 64)))
    latent_cache = centred(arg_keys[1], (2, Z, H * W), 1.0, 6.0, ((1, 4), (2, 64)))
    weight_in = centred(arg_keys[2], (3, 3, 3, C, Z), (27 * Z) ** -0.5, 0.3125, ((3, 4),))
    bias_in = centred(arg_keys[3], (C,), 0.5, 3.0, ((0, 4),), jnp.float32)
    cache_a = centred(arg_keys[4], (2, C, H * W), 1.0, 6.0, ((1, 4), (2, 64)))
    gain_a = jnp.clip(1.0 + 0.18 * jax.random.normal(arg_keys[5], (C,), jnp.float32), 0.1, 1.9)
    weight_a = centred(arg_keys[6], (3, 3, 3, C, C), (27 * C) ** -0.5, 0.0625, ((3, 4),))
    bias_a = centred(arg_keys[7], (C,), 0.5, 3.0, ((0, 4),), jnp.float32)
    cache_b = centred(arg_keys[8], (2, C, H * W), 1.0, 6.0, ((1, 4), (2, 64)))
    gain_b = jnp.clip(1.0 + 0.18 * jax.random.normal(arg_keys[9], (C,), jnp.float32), 0.1, 1.9)
    weight_b = centred(arg_keys[10], (3, 3, 3, C, C), (27 * C) ** -0.5, 0.0625, ((3, 4),))
    bias_b = centred(arg_keys[11], (C,), 0.5, 3.0, ((0, 4),), jnp.float32)
    weight_up = centred(arg_keys[12], (3, 3, CU, C), (9 * C) ** -0.5, 0.109375, ((2, 4),))
    bias_up = centred(arg_keys[13], (CU,), 0.5, 3.0, ((0, 4),), jnp.float32)
    return dict(latent=latent, latent_cache=latent_cache, weight_in=weight_in, bias_in=bias_in, cache_a=cache_a, gain_a=gain_a, weight_a=weight_a, bias_a=bias_a, cache_b=cache_b, gain_b=gain_b, weight_b=weight_b, bias_b=bias_b, weight_up=weight_up, bias_up=bias_up)


def to_grid(field):
    return field.reshape(field.shape[0], field.shape[1], H, W).transpose(0, 2, 3, 1)

def causal_conv(current, history, weight):
    joined = jnp.concatenate([history, current], 0)
    padded = jnp.pad(joined, ((0, 0), (1, 1), (1, 1), (0, 0)))
    frames, row_count, columns = (current.shape[0], current.shape[1], current.shape[2])
    outputs = weight.shape[-1]
    summed = jnp.zeros((frames * row_count * columns, outputs), jnp.float32)
    for time_tap in range(3):
        for row_tap in range(3):
            for column_tap in range(3):
                window = padded[time_tap:time_tap + frames, row_tap:row_tap + row_count, column_tap:column_tap + columns]
                summed = summed + jnp.dot(window.reshape(-1, window.shape[-1]), weight[time_tap, row_tap, column_tap], preferred_element_type=jnp.float32)
    return summed.reshape(frames, row_count, columns, outputs)

def rms_silu(features, gain_vector):
    values = features.astype(jnp.float32)
    inverse_rms = jax.lax.rsqrt(lax.optimization_barrier(jnp.mean(values * values, axis=-1, keepdims=True)) + 1e-06)
    return jax.nn.silu(values * inverse_rms * gain_vector).astype(jnp.bfloat16)

def upsample_conv(source, weight):
    doubled = jnp.repeat(jnp.repeat(source, 2, axis=1), 2, axis=2)
    padded = jnp.pad(doubled, ((0, 0), (1, 1), (1, 1), (0, 0)))
    frames, row_count, columns = (doubled.shape[0], doubled.shape[1], doubled.shape[2])
    outputs = weight.shape[-1]
    summed = jnp.zeros((frames * row_count * columns, outputs), jnp.float32)
    for row_tap in range(3):
        for column_tap in range(3):
            window = padded[:, row_tap:row_tap + row_count, column_tap:column_tap + columns]
            summed = summed + jnp.dot(window.reshape(-1, window.shape[-1]), weight[row_tap, column_tap], preferred_element_type=jnp.float32)
    return summed.reshape(frames, row_count, columns, outputs)

def reference(latent, latent_cache, weight_in, bias_in, cache_a, gain_a, weight_a, bias_a, cache_b, gain_b, weight_b, bias_b, weight_up, bias_up):
    w_in = weight_in.transpose(0, 1, 2, 4, 3)
    w_a = weight_a.transpose(0, 1, 2, 4, 3)
    w_b = weight_b.transpose(0, 1, 2, 4, 3)
    w_up = weight_up.transpose(0, 1, 3, 2)
    stem_out = (causal_conv(to_grid(latent), to_grid(latent_cache), w_in) + bias_in).astype(jnp.bfloat16)
    active_a = rms_silu(stem_out, gain_a)
    inner_out = (causal_conv(active_a, to_grid(cache_a), w_a) + bias_a).astype(jnp.bfloat16)
    active_b = rms_silu(inner_out, gain_b)
    residual_out = (stem_out.astype(jnp.float32) + causal_conv(active_b, to_grid(cache_b), w_b) + bias_b).astype(jnp.bfloat16)
    result = (upsample_conv(residual_out, w_up) + bias_up).astype(jnp.bfloat16)
    frames = result.shape[0]
    outputs = result.shape[3]
    shaped = result.reshape(frames, H, 2, W, 2, outputs).transpose(0, 5, 1, 3, 2, 4)
    return shaped.reshape(frames, outputs, 4 * H * W)
```

```python
import functools

import jax
import jax.numpy as jnp
from jax import lax
from jax.experimental import pallas as pl
from jax.experimental.pallas import tpu as pltpu
from jax.sharding import PartitionSpec as P

C = 384
W = 160
EPS = 1e-06
LANES = 256
GROUPS = 4
MESH = pl.DeviceIdType.MESH
LOW, OWN, HIGH = 0, 1, 2
F32 = jnp.float32
BF16 = jnp.bfloat16


def dot(a, b):
    return lax.dot_general(a, b, (((1,), (0,)), ((), ())), preferred_element_type=F32)


def padded(value, lanes=LANES):
    rows, count = value.shape
    return jnp.concatenate([value, jnp.zeros((rows, lanes - count), value.dtype)], axis=1)


def row_window(step, low, own, high, span):
    begin = span + (step - 1) * W - 1
    parts = []
    for piece, first in ((low, 0), (own, span), (high, 2 * span)):
        lo, hi = max(begin, first), min(begin + span + 2, first + span)
        if lo < hi:
            parts.append(piece[:, lo - first : hi - first])
    parts.append(jnp.zeros((low.shape[0], LANES - span - 2), low.dtype))
    return jnp.concatenate(parts, axis=1)


def body(
    tiles,
    span,
    latent,
    latent_cache,
    weight_in,
    bias_in,
    cache_a,
    gain_a,
    weight_a,
    bias_a,
    cache_b,
    gain_b,
    weight_b,
    bias_b,
    weight_up,
    bias_up,
    out,
    own_lat,
    lat,
    win,
    par,
    held_a,
    held_b,
    swap_a,
    swap_b,
    stem,
    maps,
    early,
    wa,
    wb,
    wu,
    up_left,
    spread,
    loc_sem,
    lat_send,
    lat_recv,
    par_send,
    par_recv,
    send_sem,
    recv_sem,
):
    tile = lax.axis_index("tile")
    chan = lax.axis_index("chan")
    mate = (tile, chan + 1 - 2 * lax.rem(chan, 2))
    far_chan = lax.rem(chan + 2, GROUPS)
    far = (tile, far_chan)
    mate_far_chan = lax.rem(mate[1] + 2, GROUPS)
    shifted = {d: lax.rem(tile + d + tiles, tiles) for d in (-2, -1, 1, 2)}
    right = (shifted[1], chan)
    left = (shifted[-1], chan)
    total = tiles * span
    start = tile * span

    def remote(src, dst, send, recv, device):
        return pltpu.make_async_remote_copy(
            src_ref=src,
            dst_ref=dst,
            send_sem=send,
            recv_sem=recv,
            device_id=device,
            device_id_type=MESH,
        )

    barrier = pltpu.get_barrier_semaphore()
    greeted = [mate, far]
    for d in (-2, -1, 1, 2):
        greeted += [(shifted[d], chan), (shifted[d], far_chan)]
    for device in greeted:
        pl.semaphore_signal(barrier, inc=1, device_id=device, device_id_type=MESH)

    local = [
        pltpu.make_async_copy(weight_a, wa, loc_sem.at[0]),
        pltpu.make_async_copy(weight_b, wb, loc_sem.at[1]),
        pltpu.make_async_copy(weight_up, wu, loc_sem.at[2]),
        pltpu.make_async_copy(cache_a, held_a.at[OWN, chan], loc_sem.at[3]),
        pltpu.make_async_copy(cache_b, held_b.at[OWN, chan], loc_sem.at[4]),
    ]
    for copy in local:
        copy.start()

    own_lat[...] = jnp.concatenate(
        [latent_cache[0].astype(F32), latent_cache[1].astype(F32), latent[0].astype(F32), latent[1].astype(F32)],
        axis=0,
    ).astype(BF16)
    win[chan] = jnp.concatenate(
        [
            weight_in[(a * 3 + b) * 3 + c].astype(F32)
            for b in range(3)
            for c in range(3)
            for a in range(3)
        ],
        axis=1,
    ).astype(BF16)
    par[chan] = jnp.concatenate(
        [
            padded(bias_in[...], 128),
            padded(gain_a[...], 128),
            padded(gain_b[...], 128),
            padded(bias_a[...], 128),
            padded(bias_b[...], 128),
            padded(bias_up[...], 128),
            jnp.zeros((2, 128), F32),
        ],
        axis=0,
    )
    pl.semaphore_wait(barrier, len(greeted))

    sends = []

    def go(copy):
        copy.start()
        sends.append(copy)

    lat[2, chan] = own_lat[...]
    index = 0
    for group in (chan, far_chan):
        for d in (-2, -1, 0, 1, 2):
            if d == 0 and group is chan:
                continue
            device = (tile if d == 0 else shifted[d], group)
            go(remote(own_lat, lat.at[2 - d, chan], lat_send.at[index], lat_recv.at[index], device))
            index += 1
    lat_count = index

    def par_copy(slot, group, device):
        go(remote(win.at[group], win.at[group], par_send.at[slot], par_recv.at[slot], device))
        go(remote(par.at[group], par.at[group], par_send.at[slot + 3], par_recv.at[slot + 3], device))

    par_copy(0, chan, far)
    par_copy(1, chan, mate)

    def exchange_copy(which, buf, number, group, slot, device, first=None):
        src = buf.at[OWN, group] if first is None else first
        return remote(
            src, buf.at[slot, group], send_sem.at[which, number], recv_sem.at[which, number], device
        )

    def send_own(which, buf, first=None):
        go(exchange_copy(which, buf, 0, chan, OWN, far, first))
        go(exchange_copy(which, buf, 2, chan, LOW, right, first))
        go(exchange_copy(which, buf, 3, chan, HIGH, left, first))
        go(exchange_copy(which, buf, 1, chan, OWN, mate, first))

    def landed(which, buf, number, slot, group):
        exchange_copy(which, buf, number, group, slot, mate).wait_recv()

    def pass_far(which, buf):
        landed(which, buf, 0, OWN, far_chan)
        go(exchange_copy(which, buf, 5, far_chan, LOW, right))
        go(exchange_copy(which, buf, 6, far_chan, HIGH, left))
        go(exchange_copy(which, buf, 4, far_chan, OWN, mate))

    def pass_rim(which, buf):
        for number, slot, group, onward in (
            (2, LOW, chan, 7),
            (3, HIGH, chan, 8),
            (5, LOW, far_chan, 9),
            (6, HIGH, far_chan, 10),
        ):
            landed(which, buf, number, slot, group)
            go(
                remote(
                    buf.at[slot, group],
                    buf.at[slot, group],
                    send_sem.at[which, onward],
                    recv_sem.at[which, onward],
                    mate,
                )
            )

    def take_mate(which, buf):
        landed(which, buf, 1, OWN, mate[1])
        landed(which, buf, 4, OWN, mate_far_chan)
        landed(which, buf, 7, LOW, mate[1])
        landed(which, buf, 8, HIGH, mate[1])
        landed(which, buf, 9, LOW, mate_far_chan)
        landed(which, buf, 10, HIGH, mate_far_chan)

    send_own(0, held_a, cache_a)
    send_own(1, held_b, cache_b)

    remote(win.at[chan], win.at[far_chan], par_send.at[0], par_recv.at[0], far).wait_recv()
    remote(par.at[chan], par.at[far_chan], par_send.at[3], par_recv.at[3], far).wait_recv()
    par_copy(2, far_chan, mate)
    for number in range(lat_count):
        remote(own_lat, lat.at[0, chan], lat_send.at[number], lat_recv.at[number], far).wait_recv()
    for slot, group in ((0, chan), (1, far_chan)):
        go(
            remote(
                lat.at[:, group],
                lat.at[:, group],
                lat_send.at[lat_count + slot],
                lat_recv.at[lat_count + slot],
                mate,
            )
        )
    pass_far(0, held_a)

    lane = lax.broadcasted_iota(jnp.int32, (1, LANES), 1)
    column = lax.rem(start + lane, W)
    inner_column = lax.rem(start + lane + (W - 1), W)
    first_column = column == 0
    last_column = column == W - 1

    def inside(step):
        cell = start + (step - 1) * W - 1 + lane
        return (cell >= 0) & (cell < total)

    remote(win.at[chan], win.at[mate[1]], par_send.at[1], par_recv.at[1], mate).wait_recv()
    remote(par.at[chan], par.at[mate[1]], par_send.at[4], par_recv.at[4], mate).wait_recv()
    remote(win.at[chan], win.at[mate_far_chan], par_send.at[2], par_recv.at[2], mate).wait_recv()
    remote(par.at[chan], par.at[mate_far_chan], par_send.at[5], par_recv.at[5], mate).wait_recv()
    columns = [par[g].T for g in range(GROUPS)]

    def full_column(number):
        return jnp.concatenate([part[: C // GROUPS, number : number + 1] for part in columns], axis=0)

    bias_in_column = full_column(0)
    gain_a_column = full_column(1)
    gain_b_column = full_column(2)
    own_columns = par[chan].T
    bias_a_column = own_columns[: C // GROUPS, 3:4]
    bias_b_column = own_columns[: C // GROUPS, 4:5]
    bias_up_column = own_columns[: C // GROUPS // 2, 5:6]

    for slot, group in ((0, mate[1]), (1, mate_far_chan)):
        remote(
            lat.at[:, group],
            lat.at[:, group],
            lat_send.at[lat_count + slot],
            lat_recv.at[lat_count + slot],
            mate,
        ).wait_recv()
    depth = GROUPS * own_lat.shape[0]
    place = lax.broadcasted_iota(jnp.int32, (depth, depth), 0)
    taken = lax.broadcasted_iota(jnp.int32, (depth, depth), 1)
    quarter = depth // 4
    small = quarter // GROUPS
    source = lax.rem(place, quarter) // small * quarter + place // quarter * small + lax.rem(place, small)
    order = jnp.where(source == taken, 1.0, 0.0).astype(BF16)
    wide = jnp.concatenate([dot(order, lat[d].reshape(depth, span)) for d in range(5)], axis=1)
    cell = start - 2 * span + lax.broadcasted_iota(jnp.int32, (1, 5 * span), 1)
    wide = jnp.where((cell >= 0) & (cell < total), wide, 0.0)
    views = {}
    for row in range(5):
        for tap in range(3):
            begin = 2 * span + (row - 2) * W + tap - 2
            view = padded(wide[:, begin : begin + span + 2])
            if tap == 0:
                view = jnp.where(inner_column == 0, 0.0, view)
            if tap == 2:
                view = jnp.where(inner_column == W - 1, 0.0, view)
            views[row, tap] = view.astype(BF16)
    stem_left = win[...].reshape(C, win.shape[2])

    def activate(values, gain_column, step):
        values = values.astype(F32)
        scale = lax.rsqrt(jnp.sum(values * values, axis=0, keepdims=True) * (1.0 / C) + EPS)
        values = values * scale * gain_column
        values = values / (1.0 + jnp.exp(-values))
        return jnp.where(inside(step), values, 0.0).astype(BF16)

    for frame in range(2):
        for step in range(3):
            right_side = jnp.concatenate(
                [
                    views[step + b, c][frame * quarter : (frame + 3) * quarter]
                    for b in range(3)
                    for c in range(3)
                ],
                axis=0,
            )
            values = (dot(stem_left, right_side) + bias_in_column).astype(BF16)
            if step == 1:
                stem[frame] = values.reshape(GROUPS, C // GROUPS, LANES)
            maps[2 + frame, step] = activate(values, gain_a_column, step)

    pass_rim(0, held_a)
    pass_far(1, held_b)
    local[3].wait()
    take_mate(0, held_a)

    def windows(buf, frame, step):
        pieces = [buf[slot, :, frame].reshape(C, span) for slot in (LOW, OWN, HIGH)]
        return row_window(step, *pieces, span)

    def load_history(buf):
        for frame in range(2):
            for step in range(3):
                values = windows(buf, frame, step)
                maps[frame, step] = jnp.where(inside(step), values, jnp.zeros_like(values))

    def taps(weight, frame, time_taps):
        acc = None
        for a in time_taps:
            for b in range(3):
                term = dot(weight[a * 3 + b], maps[frame + a, b])
                acc = term if acc is None else acc + term
        return acc

    def finish(acc, frame, bias_column, added):
        width = C // GROUPS
        middle = acc[width : 2 * width]
        if added is not None:
            middle = middle + added.astype(F32)
        result = jnp.where(first_column, 0.0, acc[:width])
        result = result + pltpu.roll(middle, LANES - 1, 1)
        result = result + jnp.where(last_column, 0.0, pltpu.roll(acc[2 * width :], LANES - 2, 1))
        return (result + bias_column).astype(BF16)[:, :span]

    load_history(held_a)
    local[0].wait()
    for frame in range(2):
        swap_a[OWN, chan, frame] = finish(taps(wa, frame, (0, 1, 2)), frame, bias_a_column, None)
    send_own(2, swap_a)

    pass_rim(1, held_b)
    local[4].wait()
    take_mate(1, held_b)
    load_history(held_b)
    local[1].wait()
    early[0] = taps(wb, 0, (0, 1))
    early[1] = taps(wb, 1, (0,))

    pass_far(2, swap_a)
    pass_rim(2, swap_a)
    take_mate(2, swap_a)
    for frame in range(2):
        for step in range(3):
            maps[2 + frame, step] = activate(windows(swap_a, frame, step), gain_b_column, step)
    for frame in range(2):
        acc = early[frame] + taps(wb, frame, (2,) if frame == 0 else (1, 2))
        swap_b[OWN, chan, frame] = finish(acc, frame, bias_b_column, stem[frame, chan])
    send_own(3, swap_b)

    local[2].wait()
    outs = C // GROUPS // 2
    row_sets = (((0,), (1, 2)), ((0, 1), (2,)))
    column_sets = ((0,), (1, 2), (0, 1), (2,))
    for p in range(2):
        for half in range(2):
            for block in range(4):
                summed = None
                for b in row_sets[p][half]:
                    for c in column_sets[block]:
                        term = wu[b * 3 + c].astype(F32)
                        summed = term if summed is None else summed + term
                up_left[p, block * outs : (block + 1) * outs, half * C : (half + 1) * C] = summed.astype(
                    BF16
                )
    half_lanes = LANES // 2
    into = lax.broadcasted_iota(jnp.int32, (4 * half_lanes, 4 * half_lanes), 1)
    whence = lax.broadcasted_iota(jnp.int32, (4 * half_lanes, 4 * half_lanes), 0)
    wanted = lax.rem(whence, half_lanes) * 4 + whence // half_lanes
    spread[...] = jnp.where(into == wanted, 1.0, 0.0).astype(BF16)

    pass_far(3, swap_b)
    pass_rim(3, swap_b)
    take_mate(3, swap_b)
    pieces = []
    for frame in range(2):
        for step in range(3):
            values = windows(swap_b, frame, step)
            maps[frame, step] = jnp.where(inside(step), values, jnp.zeros_like(values))
        quarters = []
        for p in range(2):
            acc = dot(up_left[p], maps[frame, p : p + 2].reshape(2 * C, LANES))
            even = jnp.where(first_column, 0.0, acc[:outs]) + pltpu.roll(acc[outs : 2 * outs], LANES - 1, 1)
            odd = pltpu.roll(acc[2 * outs : 3 * outs], LANES - 1, 1) + jnp.where(
                last_column, 0.0, pltpu.roll(acc[3 * outs :], LANES - 2, 1)
            )
            quarters += [(even + bias_up_column).astype(BF16), (odd + bias_up_column).astype(BF16)]
        pieces.append(quarters)
    for frame in range(2):
        quarters = pieces[frame]
        for side in range(2):
            joined = jnp.concatenate(
                [part[:, side * half_lanes : (side + 1) * half_lanes] for part in quarters], axis=1
            )
            woven = dot(joined, spread[...]).astype(BF16)
            first = side * 4 * half_lanes
            count = min(4 * half_lanes, 4 * span - first)
            out[frame, :, first : first + count] = woven[:, :count]

    for copy in sends:
        copy.wait_send()


def shards(tiles, *operands):
    (
        latent,
        latent_cache,
        weight_in,
        bias_in,
        cache_a,
        gain_a,
        weight_a,
        bias_a,
        cache_b,
        gain_b,
        weight_b,
        bias_b,
        weight_up,
        bias_up,
    ) = operands
    span = latent.shape[2]
    width = C // GROUPS
    small = latent.shape[1]
    depth = 27 * weight_in.shape[4]
    vmem = pl.BlockSpec(memory_space=pltpu.VMEM)
    hbm = pl.BlockSpec(memory_space=pl.ANY)
    block = pltpu.VMEM((3, GROUPS, 2, width, span), BF16)
    dma = pltpu.SemaphoreType.DMA
    row = lambda vector: vector.reshape(1, -1)
    return pl.pallas_call(
        functools.partial(body, tiles, span),
        out_shape=jax.ShapeDtypeStruct((2, width // 2, 4 * span), BF16),
        in_specs=[vmem, vmem, vmem, vmem, hbm, vmem, hbm, vmem, hbm, vmem, hbm, vmem, hbm, vmem],
        out_specs=vmem,
        scratch_shapes=[
            pltpu.VMEM((4 * small, span), BF16),
            pltpu.VMEM((5, GROUPS, 4 * small, span), BF16),
            pltpu.VMEM((GROUPS, width, depth), BF16),
            pltpu.VMEM((GROUPS, 8, 128), F32),
            block,
            block,
            block,
            block,
            pltpu.VMEM((2, GROUPS, width, LANES), BF16),
            pltpu.VMEM((4, 3, C, LANES), BF16),
            pltpu.VMEM((2, 3 * width, LANES), F32),
            pltpu.VMEM((9, 3 * width, C), BF16),
            pltpu.VMEM((9, 3 * width, C), BF16),
            pltpu.VMEM((9, width // 2, C), BF16),
            pltpu.VMEM((2, 4 * width // 2, 2 * C), BF16),
            pltpu.VMEM((2 * LANES, 2 * LANES), BF16),
            dma((5,)),
            dma((11,)),
            dma((11,)),
            dma((6,)),
            dma((6,)),
            dma((4, 11)),
            dma((4, 11)),
        ],
        compiler_params=pltpu.CompilerParams(
            collective_id=0, has_side_effects=True, vmem_limit_bytes=56 << 20
        ),
    )(
        latent,
        latent_cache,
        weight_in.reshape(27, width, -1),
        row(bias_in),
        cache_a,
        row(gain_a),
        weight_a.reshape(9, 3 * width, C),
        row(bias_a),
        cache_b,
        row(gain_b),
        weight_b.reshape(9, 3 * width, C),
        row(bias_b),
        weight_up.reshape(9, width // 2, C),
        row(bias_up),
    )


def solution(mesh):
    placed = (
        P(None, "chan", "tile"),
        P(None, "chan", "tile"),
        P(None, None, None, "chan", None),
        P("chan"),
        P(None, "chan", "tile"),
        P("chan"),
        P(None, None, None, "chan", None),
        P("chan"),
        P(None, "chan", "tile"),
        P("chan"),
        P(None, None, None, "chan", None),
        P("chan"),
        P(None, None, "chan", None),
        P("chan"),
    )
    return jax.shard_map(
        functools.partial(shards, mesh.shape["tile"]),
        mesh=mesh,
        in_specs=placed,
        out_specs=P(None, "chan", "tile"),
        check_vma=False,
    )
```

```python
import functools

import jax
import jax.numpy as jnp
from jax import lax
from jax.experimental import pallas as pl
from jax.experimental.pallas import tpu as pltpu
from jax.sharding import PartitionSpec as P

C = 384
W = 160
EPS = 1e-06
LANES = 256
GROUPS = 4
MESH = pl.DeviceIdType.MESH
LOW, HIGH = 0, 1
F32 = jnp.float32
BF16 = jnp.bfloat16


def dot(a, b):
    return lax.dot_general(a, b, (((1,), (0,)), ((), ())), preferred_element_type=F32)


def padded(value, lanes=LANES):
    rows, count = value.shape
    return jnp.concatenate([value, jnp.zeros((rows, lanes - count), value.dtype)], axis=1)


def rim_packs(first, second, span):
    zeros = lambda count: jnp.zeros((first.shape[0], count), first.dtype)
    last = span - W - 1
    rest = W + 1 - 128
    low = jnp.concatenate(
        [
            first[:, last : last + 128],
            second[:, last : last + 128],
            first[:, span - rest :],
            zeros(64 - rest),
            second[:, span - rest :],
            zeros(64 - rest),
        ],
        axis=1,
    )
    head = 128 - (span - W + 1)
    tail = W + 1 - head
    high = jnp.concatenate(
        [
            first[:, head : W + 1],
            zeros(128 - tail),
            second[:, head : W + 1],
            zeros(128 - tail),
            zeros(64 - head),
            second[:, :head],
            zeros(64 - head),
            first[:, :head],
        ],
        axis=1,
    )
    return low, high


def row_windows(frame, low, own, high, span):
    zeros = jnp.zeros((own.shape[0], LANES - span - 2), own.dtype)
    rest = W + 1 - 128
    head = 128 - (span - W + 1)
    tail = W + 1 - head
    at_low = 256 + 64 * frame
    at_high = 256 + 64 * (2 - frame) - head
    return (
        jnp.concatenate(
            [
                low[:, 128 * frame : 128 * frame + 128],
                low[:, at_low : at_low + rest],
                own[:, : span + 1 - W],
                zeros,
            ],
            axis=1,
        ),
        jnp.concatenate(
            [low[:, at_low + rest - 1 : at_low + rest], own, high[:, at_high : at_high + 1], zeros], axis=1
        ),
        jnp.concatenate(
            [
                own[:, W - 1 :],
                high[:, at_high : at_high + head],
                high[:, 128 * frame : 128 * frame + tail],
                zeros,
            ],
            axis=1,
        ),
    )


def body(
    tiles,
    span,
    latent,
    latent_cache,
    weight_in,
    bias_in,
    cache_a,
    gain_a,
    weight_a,
    bias_a,
    cache_b,
    gain_b,
    weight_b,
    bias_b,
    weight_up,
    bias_up,
    out,
    own_lat,
    lat,
    win,
    par,
    held_a,
    held_a_rim,
    held_b,
    held_b_rim,
    swap_a,
    swap_a_rim,
    swap_b,
    swap_b_rim,
    packs,
    stem,
    maps,
    early,
    wa,
    wb,
    wu,
    up_left,
    spread,
    loc_sem,
    lat_send,
    lat_recv,
    par_send,
    par_recv,
    send_sem,
    recv_sem,
):
    tile = lax.axis_index("tile")
    chan = lax.axis_index("chan")
    mate = (tile, chan + 1 - 2 * lax.rem(chan, 2))
    far_chan = lax.rem(chan + 2, GROUPS)
    far = (tile, far_chan)
    core = lax.rem(chan, 2)
    here = 2 * core + chan // 2
    there = 2 * core + far_chan // 2
    both = pl.ds(2 * core, 2)
    mates = pl.ds(2 - 2 * core, 2)
    shifted = {d: lax.rem(tile + d + tiles, tiles) for d in (-2, -1, 1, 2)}
    right = (shifted[1], chan)
    left = (shifted[-1], chan)
    width = C // GROUPS
    total = tiles * span
    start = tile * span

    def remote(src, dst, send, recv, device):
        return pltpu.make_async_remote_copy(
            src_ref=src,
            dst_ref=dst,
            send_sem=send,
            recv_sem=recv,
            device_id=device,
            device_id_type=MESH,
        )

    barrier = pltpu.get_barrier_semaphore()
    near = {d: (tile + d >= 0) & (tile + d < tiles) for d in (-2, -1, 1, 2)}
    met = 2
    for d in (-2, -1, 1, 2):
        met = met + 2 * near[d].astype(jnp.int32)

        @pl.when(near[d])
        def _(d=d):
            for group in (chan, far_chan):
                device = (shifted[d], group)
                pl.semaphore_signal(barrier, inc=1, device_id=device, device_id_type=MESH)

    for device in (mate, far):
        pl.semaphore_signal(barrier, inc=1, device_id=device, device_id_type=MESH)

    local = [
        pltpu.make_async_copy(weight_a, wa, loc_sem.at[0]),
        pltpu.make_async_copy(weight_b, wb, loc_sem.at[1]),
        pltpu.make_async_copy(weight_up, wu, loc_sem.at[2]),
        pltpu.make_async_copy(cache_a, held_a.at[here], loc_sem.at[3]),
        pltpu.make_async_copy(cache_b, held_b.at[here], loc_sem.at[4]),
    ]
    for number in (3, 4, 0, 1, 2):
        local[number].start()

    def pack(which, buf, waited=None):
        if waited is not None:
            local[waited].wait()
        packs[which, 0], packs[which, 1] = rim_packs(buf[here, 0], buf[here, 1], span)

    own_lat[...] = jnp.concatenate(
        [latent_cache[0].astype(F32), latent_cache[1].astype(F32), latent[0].astype(F32), latent[1].astype(F32)],
        axis=0,
    ).astype(BF16)
    taps_first = jnp.concatenate(
        [weight_in[(a * 3 + b) * 3 + c].astype(F32) for b in range(3) for c in range(3) for a in range(3)],
        axis=0,
    )
    vectors = jnp.concatenate([bias_in[...], gain_a[...], gain_b[...]], axis=0)
    first = vectors.astype(BF16).astype(F32)
    second = (vectors - first).astype(BF16).astype(F32)
    third = (vectors - first - second).astype(BF16).astype(F32)
    rows = jnp.concatenate([taps_first, first, second, third, jnp.zeros((7, width), F32)], axis=0)
    win[here] = rows.T.astype(BF16)
    own_rows = jnp.concatenate([bias_a[...], bias_b[...], jnp.zeros((6, width), F32)], axis=0)
    par[...] = padded(own_rows, 128)
    par[2:3] = padded(bias_up[...], 128)
    pack(0, held_a, 3)
    pack(1, held_b, 4)
    pl.semaphore_wait(barrier, met)

    sends = []

    def guarded(condition, act):
        if condition is None:
            act()
        else:
            pl.when(condition)(act)

    def go(copy, condition=None):
        guarded(condition, copy.start)
        sends.append((condition, copy))

    lat[here, 2] = own_lat[...]
    index = 0
    lat_waits = []
    for group in (chan, far_chan):
        for d in (-2, -1, 0, 1, 2):
            if d == 0 and group is chan:
                continue
            device = (tile if d == 0 else shifted[d], group)
            copy = remote(own_lat, lat.at[here, 2 - d], lat_send.at[index], lat_recv.at[index], device)
            go(copy, near.get(d))
            lat_waits.append((near.get(-d), copy))
            index += 1
    lat_count = index
    go(remote(win.at[here], win.at[here], par_send.at[0], par_recv.at[0], far))

    def exchange_copy(which, src, dst, number, device):
        return remote(src, dst, send_sem.at[which, number], recv_sem.at[which, number], device)

    def send_own(which, own, rim):
        low = packs.at[which, 0]
        high = packs.at[which, 1]
        go(exchange_copy(which, low, rim.at[here, LOW], 4, (shifted[1], far_chan)), near[1])
        go(exchange_copy(which, high, rim.at[here, HIGH], 5, (shifted[-1], far_chan)), near[-1])
        go(exchange_copy(which, low, rim.at[here, LOW], 2, right), near[1])
        go(exchange_copy(which, high, rim.at[here, HIGH], 3, left), near[-1])
        go(exchange_copy(which, own.at[here], own.at[here], 1, far))

    def pass_on(which, own, rim):
        for numbers, onward, refs, ref in (
            ((1,), 6, (own.at[there],), own.at[both]),
            ((2, 3), 7, (rim.at[here, LOW], rim.at[here, HIGH]), rim.at[here]),
            ((4, 5), 8, (rim.at[there, LOW], rim.at[there, HIGH]), rim.at[there]),
        ):
            for number, landed in zip(numbers, refs):
                copy = exchange_copy(which, landed, landed, number, mate)
                guarded(None if number == 1 else near[1 if number % 2 else -1], copy.wait_recv)
            go(exchange_copy(which, ref, ref, onward, mate))

    def take_mate(which, own, rim):
        for number, ref in ((6, own.at[mates]), (7, rim.at[here]), (8, rim.at[there])):
            exchange_copy(which, ref, ref, number, mate).wait_recv()

    send_own(0, held_a, held_a_rim)

    remote(win.at[here], win.at[there], par_send.at[0], par_recv.at[0], far).wait_recv()
    go(remote(win.at[both], win.at[both], par_send.at[1], par_recv.at[1], mate))
    for condition, copy in lat_waits:
        guarded(condition, copy.wait_recv)
    go(remote(lat.at[both], lat.at[both], lat_send.at[lat_count], lat_recv.at[lat_count], mate))
    pass_on(0, held_a, held_a_rim)
    send_own(1, held_b, held_b_rim)

    lane = lax.broadcasted_iota(jnp.int32, (1, LANES), 1)
    column = lax.rem(start + lane, W)
    inner_column = lax.rem(start + lane + (W - 1), W)
    first_column = column == 0
    last_column = column == W - 1

    def inside(step):
        cell = start + (step - 1) * W - 1 + lane
        return (cell >= 0) & (cell < total)

    remote(win.at[both], win.at[mates], par_send.at[1], par_recv.at[1], mate).wait_recv()
    order = (0, 2, 1, 3)
    depth = 27 * weight_in.shape[1]
    stem_left = jnp.concatenate([win[number] for number in order], axis=0)

    def full_column(number):
        parts = [stem_left[:, depth + number + 3 * k :][:, :1].astype(F32) for k in range(3)]
        return parts[0] + parts[1] + parts[2]

    bias_in_column = full_column(0)
    gain_a_column = full_column(1)
    gain_b_column = full_column(2)
    own_columns = par[...].T
    bias_a_column = own_columns[:width, 0:1]
    bias_b_column = own_columns[:width, 1:2]
    bias_up_column = own_columns[: width // 2, 2:3]
    stem_left = stem_left[:, :depth]

    remote(lat.at[both], lat.at[mates], lat_send.at[lat_count], lat_recv.at[lat_count], mate).wait_recv()
    depth = GROUPS * own_lat.shape[0]
    place = lax.broadcasted_iota(jnp.int32, (depth, depth), 0)
    taken = lax.broadcasted_iota(jnp.int32, (depth, depth), 1)
    quarter = depth // 4
    small = quarter // GROUPS
    source = lax.rem(place, quarter) // small * quarter + place // quarter * small + lax.rem(place, small)
    sorter = jnp.where(source == taken, 1.0, 0.0).astype(BF16)
    wide = jnp.concatenate(
        [dot(sorter, jnp.concatenate([lat[number, d] for number in order], axis=0)) for d in range(5)], axis=1
    )
    cell = start - 2 * span + lax.broadcasted_iota(jnp.int32, (1, 5 * span), 1)
    wide = jnp.where((cell >= 0) & (cell < total), wide, 0.0)
    views = {}
    for row in range(5):
        for tap in range(3):
            begin = 2 * span + (row - 2) * W + tap - 2
            view = padded(wide[:, begin : begin + span + 2])
            if tap == 0:
                view = jnp.where(inner_column == 0, 0.0, view)
            if tap == 2:
                view = jnp.where(inner_column == W - 1, 0.0, view)
            views[row, tap] = view.astype(BF16)

    def activate(values, gain_column, step):
        values = values.astype(F32)
        scale = lax.rsqrt(jnp.sum(values * values, axis=0, keepdims=True) * (1.0 / C) + EPS)
        values = values * scale * gain_column
        values = values / (1.0 + jnp.exp(-values))
        return jnp.where(inside(step), values, 0.0).astype(BF16)

    for frame in range(2):
        for step in range(3):
            right_side = jnp.concatenate(
                [
                    views[step + b, c][frame * quarter : (frame + 3) * quarter]
                    for b in range(3)
                    for c in range(3)
                ],
                axis=0,
            )
            values = (dot(stem_left, right_side) + bias_in_column).astype(BF16)
            if step == 1:
                stem[frame] = values.reshape(GROUPS, C // GROUPS, LANES)
            maps[2 + frame, step] = activate(values, gain_a_column, step)

    take_mate(0, held_a, held_a_rim)

    def windows(own, rim, frame):
        low, high = (jnp.concatenate([rim[number, side] for number in order], axis=0) for side in (LOW, HIGH))
        middle = jnp.concatenate([own[number, frame] for number in order], axis=0)
        return row_windows(frame, low, middle, high, span)

    def load_windows(own, rim):
        for frame in range(2):
            for step, values in enumerate(windows(own, rim, frame)):
                maps[frame, step] = jnp.where(inside(step), values, jnp.zeros_like(values))

    def taps(weight, frame, time_taps):
        acc = None
        for a in time_taps:
            for b in range(3):
                term = dot(weight[a * 3 + b], maps[frame + a, b])
                acc = term if acc is None else acc + term
        return acc

    def finish(acc, frame, bias_column, added):
        middle = acc[width : 2 * width]
        if added is not None:
            middle = middle + added.astype(F32)
        result = jnp.where(first_column, 0.0, acc[:width])
        result = result + pltpu.roll(middle, LANES - 1, 1)
        result = result + jnp.where(last_column, 0.0, pltpu.roll(acc[2 * width :], LANES - 2, 1))
        return (result + bias_column).astype(BF16)[:, :span]

    load_windows(held_a, held_a_rim)
    local[0].wait()
    for frame in range(2):
        swap_a[here, frame] = finish(taps(wa, frame, (0, 1, 2)), frame, bias_a_column, None)
    pack(2, swap_a)
    send_own(2, swap_a, swap_a_rim)

    pass_on(1, held_b, held_b_rim)
    take_mate(1, held_b, held_b_rim)
    load_windows(held_b, held_b_rim)
    local[1].wait()
    early[0] = taps(wb, 0, (0, 1))
    early[1] = taps(wb, 1, (0,))

    pass_on(2, swap_a, swap_a_rim)
    take_mate(2, swap_a, swap_a_rim)
    for frame in range(2):
        for step, values in enumerate(windows(swap_a, swap_a_rim, frame)):
            maps[2 + frame, step] = activate(values, gain_b_column, step)
    for frame in range(2):
        acc = early[frame] + taps(wb, frame, (2,) if frame == 0 else (1, 2))
        swap_b[here, frame] = finish(acc, frame, bias_b_column, stem[frame, chan])
    pack(3, swap_b)
    send_own(3, swap_b, swap_b_rim)

    local[2].wait()
    outs = C // GROUPS // 2
    row_sets = (((0,), (1, 2)), ((0, 1), (2,)))
    column_sets = ((0,), (1, 2), (0, 1), (2,))
    for p in range(2):
        for half in range(2):
            for block in range(4):
                summed = None
                for b in row_sets[p][half]:
                    for c in column_sets[block]:
                        term = wu[b * 3 + c].astype(F32)
                        summed = term if summed is None else summed + term
                up_left[p, block * outs : (block + 1) * outs, half * C : (half + 1) * C] = summed.astype(
                    BF16
                )
    half_lanes = LANES // 2
    into = lax.broadcasted_iota(jnp.int32, (4 * half_lanes, 4 * half_lanes), 1)
    whence = lax.broadcasted_iota(jnp.int32, (4 * half_lanes, 4 * half_lanes), 0)
    wanted = lax.rem(whence, half_lanes) * 4 + whence // half_lanes
    spread[...] = jnp.where(into == wanted, 1.0, 0.0).astype(BF16)

    pass_on(3, swap_b, swap_b_rim)
    take_mate(3, swap_b, swap_b_rim)
    load_windows(swap_b, swap_b_rim)
    pieces = []
    for frame in range(2):
        quarters = []
        for p in range(2):
            acc = dot(up_left[p], maps[frame, p : p + 2].reshape(2 * C, LANES))
            even = jnp.where(first_column, 0.0, acc[:outs]) + pltpu.roll(acc[outs : 2 * outs], LANES - 1, 1)
            odd = pltpu.roll(acc[2 * outs : 3 * outs], LANES - 1, 1) + jnp.where(
                last_column, 0.0, pltpu.roll(acc[3 * outs :], LANES - 2, 1)
            )
            quarters += [(even + bias_up_column).astype(BF16), (odd + bias_up_column).astype(BF16)]
        pieces.append(quarters)
    for frame in range(2):
        quarters = pieces[frame]
        for side in range(2):
            joined = jnp.concatenate(
                [part[:, side * half_lanes : (side + 1) * half_lanes] for part in quarters], axis=1
            )
            woven = dot(joined, spread[...]).astype(BF16)
            first = side * 4 * half_lanes
            count = min(4 * half_lanes, 4 * span - first)
            out[frame, :, first : first + count] = woven[:, :count]

    for condition, copy in sends:
        guarded(condition, copy.wait_send)


def shards(tiles, *operands):
    (
        latent,
        latent_cache,
        weight_in,
        bias_in,
        cache_a,
        gain_a,
        weight_a,
        bias_a,
        cache_b,
        gain_b,
        weight_b,
        bias_b,
        weight_up,
        bias_up,
    ) = operands
    span = latent.shape[2]
    width = C // GROUPS
    small = latent.shape[1]
    depth = 27 * weight_in.shape[4]
    vmem = pl.BlockSpec(memory_space=pltpu.VMEM)
    hbm = pl.BlockSpec(memory_space=pl.ANY)
    block = pltpu.VMEM((GROUPS, 2, width, span), BF16)
    rim = pltpu.VMEM((GROUPS, 2, width, 384), BF16)
    dma = pltpu.SemaphoreType.DMA
    row = lambda vector: vector.reshape(1, -1)
    return pl.pallas_call(
        functools.partial(body, tiles, span),
        out_shape=jax.ShapeDtypeStruct((2, width // 2, 4 * span), BF16),
        in_specs=[vmem, vmem, vmem, vmem, hbm, vmem, hbm, vmem, hbm, vmem, hbm, vmem, hbm, vmem],
        out_specs=vmem,
        scratch_shapes=[
            pltpu.VMEM((4 * small, span), BF16),
            pltpu.VMEM((GROUPS, 5, 4 * small, span), BF16),
            pltpu.VMEM((GROUPS, width, depth + 16), BF16),
            pltpu.VMEM((8, 128), F32),
            block,
            rim,
            block,
            rim,
            block,
            rim,
            block,
            rim,
            pltpu.VMEM((4, 2, width, 384), BF16),
            pltpu.VMEM((2, GROUPS, width, LANES), BF16),
            pltpu.VMEM((4, 3, C, LANES), BF16),
            pltpu.VMEM((2, 3 * width, LANES), F32),
            pltpu.VMEM((9, 3 * width, C), BF16),
            pltpu.VMEM((9, 3 * width, C), BF16),
            pltpu.VMEM((9, width // 2, C), BF16),
            pltpu.VMEM((2, 4 * width // 2, 2 * C), BF16),
            pltpu.VMEM((2 * LANES, 2 * LANES), BF16),
            dma((5,)),
            dma((10,)),
            dma((10,)),
            dma((2,)),
            dma((2,)),
            dma((4, 9)),
            dma((4, 9)),
        ],
        compiler_params=pltpu.CompilerParams(
            collective_id=0, has_side_effects=True, vmem_limit_bytes=56 << 20
        ),
    )(
        latent,
        latent_cache,
        weight_in.swapaxes(3, 4).reshape(27, -1, width),
        row(bias_in),
        cache_a,
        row(gain_a),
        weight_a.reshape(9, 3 * width, C),
        row(bias_a),
        cache_b,
        row(gain_b),
        weight_b.reshape(9, 3 * width, C),
        row(bias_b),
        weight_up.reshape(9, width // 2, C),
        row(bias_up),
    )


def solution(mesh):
    placed = (
        P(None, "chan", "tile"),
        P(None, "chan", "tile"),
        P(None, None, None, "chan", None),
        P("chan"),
        P(None, "chan", "tile"),
        P("chan"),
        P(None, None, None, "chan", None),
        P("chan"),
        P(None, "chan", "tile"),
        P("chan"),
        P(None, None, None, "chan", None),
        P("chan"),
        P(None, None, "chan", None),
        P("chan"),
    )
    return jax.shard_map(
        functools.partial(shards, mesh.shape["tile"]),
        mesh=mesh,
        in_specs=placed,
        out_specs=P(None, "chan", "tile"),
        check_vma=False,
    )
```

```python
import functools

import jax
import jax.numpy as jnp
from jax import lax
from jax.experimental import pallas as pl
from jax.experimental.pallas import tpu as pltpu
from jax.sharding import PartitionSpec as P

C = 384
W = 160
EPS = 1e-06
LANES = 256
GROUPS = 4
MESH = pl.DeviceIdType.MESH
LOW, HIGH = 0, 1
F32 = jnp.float32
BF16 = jnp.bfloat16


def dot(a, b):
    return lax.dot_general(a, b, (((1,), (0,)), ((), ())), preferred_element_type=F32)


def padded(value, lanes=LANES):
    rows, count = value.shape
    return jnp.concatenate([value, jnp.zeros((rows, lanes - count), value.dtype)], axis=1)


def rim_packs(first, second, span):
    zeros = lambda count: jnp.zeros((first.shape[0], count), first.dtype)
    last = span - W - 1
    rest = W + 1 - 128
    low = jnp.concatenate(
        [
            first[:, last : last + 128],
            second[:, last : last + 128],
            first[:, span - rest :],
            zeros(64 - rest),
            second[:, span - rest :],
            zeros(64 - rest),
        ],
        axis=1,
    )
    head = 128 - (span - W + 1)
    tail = W + 1 - head
    high = jnp.concatenate(
        [
            first[:, head : W + 1],
            zeros(128 - tail),
            second[:, head : W + 1],
            zeros(128 - tail),
            zeros(64 - head),
            second[:, :head],
            zeros(64 - head),
            first[:, :head],
        ],
        axis=1,
    )
    return low, high


def row_windows(frame, low, own, high, span):
    zeros = jnp.zeros((own.shape[0], LANES - span - 2), own.dtype)
    rest = W + 1 - 128
    head = 128 - (span - W + 1)
    tail = W + 1 - head
    at_low = 256 + 64 * frame
    at_high = 256 + 64 * (2 - frame) - head
    return (
        jnp.concatenate(
            [
                low[:, 128 * frame : 128 * frame + 128],
                low[:, at_low : at_low + rest],
                own[:, : span + 1 - W],
                zeros,
            ],
            axis=1,
        ),
        jnp.concatenate(
            [low[:, at_low + rest - 1 : at_low + rest], own, high[:, at_high : at_high + 1], zeros], axis=1
        ),
        jnp.concatenate(
            [
                own[:, W - 1 :],
                high[:, at_high : at_high + head],
                high[:, 128 * frame : 128 * frame + tail],
                zeros,
            ],
            axis=1,
        ),
    )


def body(
    tiles,
    span,
    latent,
    latent_cache,
    weight_in,
    bias_in,
    cache_a,
    gain_a,
    weight_a,
    bias_a,
    cache_b,
    gain_b,
    weight_b,
    bias_b,
    weight_up,
    bias_up,
    out,
    own_lat,
    lat,
    win,
    par,
    held_a,
    held_a_rim,
    held_b,
    held_b_rim,
    swap_a,
    swap_a_rim,
    swap_b,
    swap_b_rim,
    packs,
    stem,
    maps,
    early,
    wa,
    wb,
    wu,
    up_left,
    spread,
    loc_sem,
    lat_send,
    lat_recv,
    par_send,
    par_recv,
    send_sem,
    recv_sem,
):
    tile = lax.axis_index("tile")
    chan = lax.axis_index("chan")
    mate = (tile, chan + 1 - 2 * lax.rem(chan, 2))
    far_chan = lax.rem(chan + 2, GROUPS)
    far = (tile, far_chan)
    core = lax.rem(chan, 2)
    here = 2 * core + chan // 2
    there = 2 * core + far_chan // 2
    both = pl.ds(2 * core, 2)
    mates = pl.ds(2 - 2 * core, 2)
    shifted = {d: lax.rem(tile + d + tiles, tiles) for d in (-2, -1, 1, 2)}
    right = (shifted[1], chan)
    left = (shifted[-1], chan)
    width = C // GROUPS
    total = tiles * span
    start = tile * span

    def remote(src, dst, send, recv, device):
        return pltpu.make_async_remote_copy(
            src_ref=src,
            dst_ref=dst,
            send_sem=send,
            recv_sem=recv,
            device_id=device,
            device_id_type=MESH,
        )

    barrier = pltpu.get_barrier_semaphore()
    near = {d: (tile + d >= 0) & (tile + d < tiles) for d in (-2, -1, 1, 2)}
    met = 2
    for d in (-1, 1):
        met = met + 2 * near[d].astype(jnp.int32)

        @pl.when(near[d])
        def _(d=d):
            for group in (chan, far_chan):
                device = (shifted[d], group)
                pl.semaphore_signal(barrier, inc=1, device_id=device, device_id_type=MESH)

    for device in (mate, far):
        pl.semaphore_signal(barrier, inc=1, device_id=device, device_id_type=MESH)

    local = [
        pltpu.make_async_copy(weight_a, wa, loc_sem.at[0]),
        pltpu.make_async_copy(weight_b, wb, loc_sem.at[1]),
        pltpu.make_async_copy(weight_up, wu, loc_sem.at[2]),
        pltpu.make_async_copy(cache_a, held_a.at[here], loc_sem.at[3]),
        pltpu.make_async_copy(cache_b, held_b.at[here], loc_sem.at[4]),
    ]
    for number in (3, 4, 0, 1, 2):
        local[number].start()

    def pack(which, buf, waited=None):
        if waited is not None:
            local[waited].wait()
        packs[which, 0], packs[which, 1] = rim_packs(buf[here, 0], buf[here, 1], span)

    own_lat[...] = jnp.concatenate(
        [latent_cache[0].astype(F32), latent_cache[1].astype(F32), latent[0].astype(F32), latent[1].astype(F32)],
        axis=0,
    ).astype(BF16)
    taps_first = jnp.concatenate(
        [weight_in[(a * 3 + b) * 3 + c].astype(F32) for b in range(3) for c in range(3) for a in range(3)],
        axis=0,
    )
    vectors = jnp.concatenate([bias_in[...], gain_a[...], gain_b[...]], axis=0)
    first = vectors.astype(BF16).astype(F32)
    second = (vectors - first).astype(BF16).astype(F32)
    third = (vectors - first - second).astype(BF16).astype(F32)
    rows = jnp.concatenate([taps_first, first, second, third, jnp.zeros((7, width), F32)], axis=0)
    win[here] = rows.T.astype(BF16)
    pack(0, held_a, 3)
    pl.semaphore_wait(barrier, met)

    sends = []

    def guarded(condition, act):
        if condition is None:
            act()
        else:
            pl.when(condition)(act)

    def go(copy, condition=None):
        guarded(condition, copy.start)
        sends.append((condition, copy))

    lat[here, 2] = own_lat[...]
    lat_waits = []
    for index, (d, group) in enumerate(((1, chan), (-1, chan), (1, far_chan), (-1, far_chan), (0, far_chan))):
        device = (shifted[d] if d else tile, group)
        copy = remote(own_lat, lat.at[here, 2 - d], lat_send.at[index], lat_recv.at[index], device)
        go(copy, near.get(d))
        lat_waits.append((near.get(-d), copy))
    go(remote(win.at[here], win.at[here], par_send.at[0], par_recv.at[0], far))

    def exchange_copy(which, src, dst, number, device):
        return remote(src, dst, send_sem.at[which, number], recv_sem.at[which, number], device)

    def send_own(which, own, rim):
        low = packs.at[which, 0]
        high = packs.at[which, 1]
        go(exchange_copy(which, low, rim.at[here, LOW], 4, (shifted[1], far_chan)), near[1])
        go(exchange_copy(which, high, rim.at[here, HIGH], 5, (shifted[-1], far_chan)), near[-1])
        go(exchange_copy(which, low, rim.at[here, LOW], 2, right), near[1])
        go(exchange_copy(which, high, rim.at[here, HIGH], 3, left), near[-1])
        go(exchange_copy(which, own.at[here], own.at[here], 1, far))

    def pass_on(which, own, rim):
        for numbers, onward, refs, ref in (
            ((1,), 6, (own.at[there],), own.at[both]),
            ((2, 3), 7, (rim.at[here, LOW], rim.at[here, HIGH]), rim.at[here]),
            ((4, 5), 8, (rim.at[there, LOW], rim.at[there, HIGH]), rim.at[there]),
        ):
            for number, landed in zip(numbers, refs):
                copy = exchange_copy(which, landed, landed, number, mate)
                guarded(None if number == 1 else near[1 if number % 2 else -1], copy.wait_recv)
            go(exchange_copy(which, ref, ref, onward, mate))

    def take_mate(which, own, rim):
        for number, ref in ((6, own.at[mates]), (7, rim.at[here]), (8, rim.at[there])):
            exchange_copy(which, ref, ref, number, mate).wait_recv()

    send_own(0, held_a, held_a_rim)

    between = near[-1] & near[1]
    for d in (1, -1):
        for number in ((0, 2) if d == 1 else (1, 3)):
            guarded(lat_waits[number][0], lat_waits[number][1].wait_recv)
        copy = remote(
            lat.at[both, 2 - d], lat.at[both, 2 - 2 * d], lat_send.at[5 + (d < 0)], lat_recv.at[5 + (d < 0)],
            (shifted[d], chan),
        )
        go(copy, between)
        lat_waits.append((near[-2 * d], copy))
    remote(win.at[here], win.at[there], par_send.at[0], par_recv.at[0], far).wait_recv()
    go(remote(win.at[both], win.at[both], par_send.at[1], par_recv.at[1], mate))
    for condition, copy in lat_waits[4:]:
        guarded(condition, copy.wait_recv)
    go(remote(lat.at[both], lat.at[both], lat_send.at[7], lat_recv.at[7], mate))
    pass_on(0, held_a, held_a_rim)
    pack(1, held_b, 4)
    send_own(1, held_b, held_b_rim)

    lane = lax.broadcasted_iota(jnp.int32, (1, LANES), 1)
    column = lax.rem(start + lane, W)
    inner_column = lax.rem(start + lane + (W - 1), W)
    first_column = column == 0
    last_column = column == W - 1

    def inside(step):
        cell = start + (step - 1) * W - 1 + lane
        return (cell >= 0) & (cell < total)

    remote(win.at[both], win.at[mates], par_send.at[1], par_recv.at[1], mate).wait_recv()
    order = (0, 2, 1, 3)
    depth = 27 * weight_in.shape[1]
    stem_left = jnp.concatenate([win[number] for number in order], axis=0)

    def full_column(number):
        parts = [stem_left[:, depth + number + 3 * k :][:, :1].astype(F32) for k in range(3)]
        return parts[0] + parts[1] + parts[2]

    bias_in_column = full_column(0)
    gain_a_column = full_column(1)
    gain_b_column = full_column(2)
    own_rows = jnp.concatenate([bias_a[...], bias_b[...], jnp.zeros((6, width), F32)], axis=0)
    par[...] = padded(own_rows, 128)
    par[2:3] = padded(bias_up[...], 128)
    own_columns = par[...].T
    bias_a_column = own_columns[:width, 0:1]
    bias_b_column = own_columns[:width, 1:2]
    bias_up_column = own_columns[: width // 2, 2:3]
    stem_left = stem_left[:, :depth]

    remote(lat.at[both], lat.at[mates], lat_send.at[7], lat_recv.at[7], mate).wait_recv()
    depth = GROUPS * own_lat.shape[0]
    place = lax.broadcasted_iota(jnp.int32, (depth, depth), 0)
    taken = lax.broadcasted_iota(jnp.int32, (depth, depth), 1)
    quarter = depth // 4
    small = quarter // GROUPS
    source = lax.rem(place, quarter) // small * quarter + place // quarter * small + lax.rem(place, small)
    sorter = jnp.where(source == taken, 1.0, 0.0).astype(BF16)
    wide = jnp.concatenate(
        [dot(sorter, jnp.concatenate([lat[number, d] for number in order], axis=0)) for d in range(5)], axis=1
    )
    cell = start - 2 * span + lax.broadcasted_iota(jnp.int32, (1, 5 * span), 1)
    wide = jnp.where((cell >= 0) & (cell < total), wide, 0.0)
    views = {}
    for row in range(5):
        for tap in range(3):
            begin = 2 * span + (row - 2) * W + tap - 2
            view = padded(wide[:, begin : begin + span + 2])
            if tap == 0:
                view = jnp.where(inner_column == 0, 0.0, view)
            if tap == 2:
                view = jnp.where(inner_column == W - 1, 0.0, view)
            views[row, tap] = view.astype(BF16)

    def activate(values, gain_column, step):
        values = values.astype(F32)
        scale = lax.rsqrt(jnp.sum(values * values, axis=0, keepdims=True) * (1.0 / C) + EPS)
        values = values * scale * gain_column
        values = values / (1.0 + jnp.exp(-values))
        return jnp.where(inside(step), values, 0.0).astype(BF16)

    for frame in range(2):
        for step in range(3):
            right_side = jnp.concatenate(
                [
                    views[step + b, c][frame * quarter : (frame + 3) * quarter]
                    for b in range(3)
                    for c in range(3)
                ],
                axis=0,
            )
            values = (dot(stem_left, right_side) + bias_in_column).astype(BF16)
            if step == 1:
                stem[frame] = values.reshape(GROUPS, C // GROUPS, LANES)
            maps[2 + frame, step] = activate(values, gain_a_column, step)

    def windows(own, rim, frame):
        low, high = (jnp.concatenate([rim[number, side] for number in order], axis=0) for side in (LOW, HIGH))
        middle = jnp.concatenate([own[number, frame] for number in order], axis=0)
        return row_windows(frame, low, middle, high, span)

    def load_windows(own, rim):
        for frame in range(2):
            for step, values in enumerate(windows(own, rim, frame)):
                maps[frame, step] = jnp.where(inside(step), values, jnp.zeros_like(values))

    def taps(weight, frame, time_taps):
        acc = None
        for a in time_taps:
            for b in range(3):
                term = dot(weight[a * 3 + b], maps[frame + a, b])
                acc = term if acc is None else acc + term
        return acc

    def finish(acc, frame, bias_column, added):
        middle = acc[width : 2 * width]
        if added is not None:
            middle = middle + added.astype(F32)
        result = jnp.where(first_column, 0.0, acc[:width])
        result = result + pltpu.roll(middle, LANES - 1, 1)
        result = result + jnp.where(last_column, 0.0, pltpu.roll(acc[2 * width :], LANES - 2, 1))
        return (result + bias_column).astype(BF16)[:, :span]

    local[0].wait()
    early[0] = taps(wa, 0, (2,))
    early[1] = taps(wa, 1, (1, 2))
    take_mate(0, held_a, held_a_rim)
    load_windows(held_a, held_a_rim)
    for frame in range(2):
        acc = early[frame] + taps(wa, frame, (0, 1) if frame == 0 else (0,))
        swap_a[here, frame] = finish(acc, frame, bias_a_column, None)
    pack(2, swap_a)
    send_own(2, swap_a, swap_a_rim)

    pass_on(1, held_b, held_b_rim)
    take_mate(1, held_b, held_b_rim)
    load_windows(held_b, held_b_rim)
    local[1].wait()
    early[0] = taps(wb, 0, (0, 1))
    early[1] = taps(wb, 1, (0,))

    pass_on(2, swap_a, swap_a_rim)
    take_mate(2, swap_a, swap_a_rim)
    for frame in range(2):
        for step, values in enumerate(windows(swap_a, swap_a_rim, frame)):
            maps[2 + frame, step] = activate(values, gain_b_column, step)
    for frame in range(2):
        acc = early[frame] + taps(wb, frame, (2,) if frame == 0 else (1, 2))
        swap_b[here, frame] = finish(acc, frame, bias_b_column, stem[frame, chan])
    pack(3, swap_b)
    send_own(3, swap_b, swap_b_rim)

    local[2].wait()
    outs = C // GROUPS // 2
    row_sets = (((0,), (1, 2)), ((0, 1), (2,)))
    column_sets = ((0,), (1, 2), (0, 1), (2,))
    for p in range(2):
        for half in range(2):
            for block in range(4):
                summed = None
                for b in row_sets[p][half]:
                    for c in column_sets[block]:
                        term = wu[b * 3 + c].astype(F32)
                        summed = term if summed is None else summed + term
                up_left[p, block * outs : (block + 1) * outs, half * C : (half + 1) * C] = summed.astype(
                    BF16
                )
    half_lanes = LANES // 2
    into = lax.broadcasted_iota(jnp.int32, (4 * half_lanes, 4 * half_lanes), 1)
    whence = lax.broadcasted_iota(jnp.int32, (4 * half_lanes, 4 * half_lanes), 0)
    wanted = lax.rem(whence, half_lanes) * 4 + whence // half_lanes
    spread[...] = jnp.where(into == wanted, 1.0, 0.0).astype(BF16)

    pass_on(3, swap_b, swap_b_rim)
    take_mate(3, swap_b, swap_b_rim)
    load_windows(swap_b, swap_b_rim)
    pieces = []
    for frame in range(2):
        quarters = []
        for p in range(2):
            acc = dot(up_left[p], maps[frame, p : p + 2].reshape(2 * C, LANES))
            even = jnp.where(first_column, 0.0, acc[:outs]) + pltpu.roll(acc[outs : 2 * outs], LANES - 1, 1)
            odd = pltpu.roll(acc[2 * outs : 3 * outs], LANES - 1, 1) + jnp.where(
                last_column, 0.0, pltpu.roll(acc[3 * outs :], LANES - 2, 1)
            )
            quarters += [(even + bias_up_column).astype(BF16), (odd + bias_up_column).astype(BF16)]
        pieces.append(quarters)
    for frame in range(2):
        quarters = pieces[frame]
        for side in range(2):
            joined = jnp.concatenate(
                [part[:, side * half_lanes : (side + 1) * half_lanes] for part in quarters], axis=1
            )
            woven = dot(joined, spread[...]).astype(BF16)
            first = side * 4 * half_lanes
            count = min(4 * half_lanes, 4 * span - first)
            out[frame, :, first : first + count] = woven[:, :count]

    for condition, copy in sends:
        guarded(condition, copy.wait_send)


def shards(tiles, *operands):
    (
        latent,
        latent_cache,
        weight_in,
        bias_in,
        cache_a,
        gain_a,
        weight_a,
        bias_a,
        cache_b,
        gain_b,
        weight_b,
        bias_b,
        weight_up,
        bias_up,
    ) = operands
    span = latent.shape[2]
    width = C // GROUPS
    small = latent.shape[1]
    depth = 27 * weight_in.shape[4]
    vmem = pl.BlockSpec(memory_space=pltpu.VMEM)
    hbm = pl.BlockSpec(memory_space=pl.ANY)
    block = pltpu.VMEM((GROUPS, 2, width, span), BF16)
    rim = pltpu.VMEM((GROUPS, 2, width, 384), BF16)
    dma = pltpu.SemaphoreType.DMA
    row = lambda vector: vector.reshape(1, -1)
    return pl.pallas_call(
        functools.partial(body, tiles, span),
        out_shape=jax.ShapeDtypeStruct((2, width // 2, 4 * span), BF16),
        in_specs=[vmem, vmem, vmem, vmem, hbm, vmem, hbm, vmem, hbm, vmem, hbm, vmem, hbm, vmem],
        out_specs=vmem,
        scratch_shapes=[
            pltpu.VMEM((4 * small, span), BF16),
            pltpu.VMEM((GROUPS, 5, 4 * small, span), BF16),
            pltpu.VMEM((GROUPS, width, depth + 16), BF16),
            pltpu.VMEM((8, 128), F32),
            block,
            rim,
            block,
            rim,
            block,
            rim,
            block,
            rim,
            pltpu.VMEM((4, 2, width, 384), BF16),
            pltpu.VMEM((2, GROUPS, width, LANES), BF16),
            pltpu.VMEM((4, 3, C, LANES), BF16),
            pltpu.VMEM((2, 3 * width, LANES), F32),
            pltpu.VMEM((9, 3 * width, C), BF16),
            pltpu.VMEM((9, 3 * width, C), BF16),
            pltpu.VMEM((9, width // 2, C), BF16),
            pltpu.VMEM((2, 4 * width // 2, 2 * C), BF16),
            pltpu.VMEM((2 * LANES, 2 * LANES), BF16),
            dma((5,)),
            dma((8,)),
            dma((8,)),
            dma((2,)),
            dma((2,)),
            dma((4, 9)),
            dma((4, 9)),
        ],
        compiler_params=pltpu.CompilerParams(
            collective_id=0, has_side_effects=True, vmem_limit_bytes=56 << 20
        ),
    )(
        latent,
        latent_cache,
        weight_in.swapaxes(3, 4).reshape(27, -1, width),
        row(bias_in),
        cache_a,
        row(gain_a),
        weight_a.reshape(9, 3 * width, C),
        row(bias_a),
        cache_b,
        row(gain_b),
        weight_b.reshape(9, 3 * width, C),
        row(bias_b),
        weight_up.reshape(9, width // 2, C),
        row(bias_up),
    )


def solution(mesh):
    placed = (
        P(None, "chan", "tile"),
        P(None, "chan", "tile"),
        P(None, None, None, "chan", None),
        P("chan"),
        P(None, "chan", "tile"),
        P("chan"),
        P(None, None, None, "chan", None),
        P("chan"),
        P(None, "chan", "tile"),
        P("chan"),
        P(None, None, None, "chan", None),
        P("chan"),
        P(None, None, "chan", None),
        P("chan"),
    )
    return jax.shard_map(
        functools.partial(shards, mesh.shape["tile"]),
        mesh=mesh,
        in_specs=placed,
        out_specs=P(None, "chan", "tile"),
        check_vma=False,
    )
```

```python
import functools

import jax
import jax.numpy as jnp
from jax import lax
from jax.experimental import pallas as pl
from jax.experimental.pallas import tpu as pltpu
from jax.sharding import PartitionSpec as P

C = 384
W = 160
EPS = 1e-06
LANES = 256
GROUPS = 4
MESH = pl.DeviceIdType.MESH
LOW, HIGH = 0, 1
F32 = jnp.float32
BF16 = jnp.bfloat16


def dot(a, b):
    return lax.dot_general(a, b, (((1,), (0,)), ((), ())), preferred_element_type=F32)


def padded(value, lanes=LANES):
    rows, count = value.shape
    return jnp.concatenate([value, jnp.zeros((rows, lanes - count), value.dtype)], axis=1)


def rim_packs(first, second, span):
    zeros = lambda count: jnp.zeros((first.shape[0], count), first.dtype)
    last = span - W - 1
    rest = W + 1 - 128
    low = jnp.concatenate(
        [
            first[:, last : last + 128],
            second[:, last : last + 128],
            first[:, span - rest :],
            zeros(64 - rest),
            second[:, span - rest :],
            zeros(64 - rest),
        ],
        axis=1,
    )
    head = 128 - (span - W + 1)
    tail = W + 1 - head
    high = jnp.concatenate(
        [
            first[:, head : W + 1],
            zeros(128 - tail),
            second[:, head : W + 1],
            zeros(128 - tail),
            zeros(64 - head),
            second[:, :head],
            zeros(64 - head),
            first[:, :head],
        ],
        axis=1,
    )
    return low, high


def row_windows(frame, low, own, high, span):
    zeros = jnp.zeros((own.shape[0], LANES - span - 2), own.dtype)
    rest = W + 1 - 128
    head = 128 - (span - W + 1)
    tail = W + 1 - head
    at_low = 256 + 64 * frame
    at_high = 256 + 64 * (2 - frame) - head
    return (
        jnp.concatenate(
            [
                low[:, 128 * frame : 128 * frame + 128],
                low[:, at_low : at_low + rest],
                own[:, : span + 1 - W],
                zeros,
            ],
            axis=1,
        ),
        jnp.concatenate(
            [low[:, at_low + rest - 1 : at_low + rest], own, high[:, at_high : at_high + 1], zeros], axis=1
        ),
        jnp.concatenate(
            [
                own[:, W - 1 :],
                high[:, at_high : at_high + head],
                high[:, 128 * frame : 128 * frame + tail],
                zeros,
            ],
            axis=1,
        ),
    )


def body(
    tiles,
    span,
    latent_hbm,
    latent_cache_hbm,
    weight_in_hbm,
    bias_in_hbm,
    cache_a,
    gain_a_hbm,
    weight_a,
    bias_a_hbm,
    cache_b,
    gain_b_hbm,
    weight_b,
    bias_b_hbm,
    weight_up,
    bias_up_hbm,
    out,
    latent,
    latent_cache,
    weight_in,
    bias_in,
    gain_a,
    bias_a,
    gain_b,
    bias_b,
    bias_up,
    own_lat,
    lat,
    win,
    par,
    held_a,
    held_a_rim,
    held_b,
    held_b_rim,
    swap_a,
    swap_a_rim,
    swap_b,
    swap_b_rim,
    packs,
    stem,
    maps,
    early,
    wa,
    wb,
    wu,
    up_left,
    spread,
    loc_sem,
    lat_send,
    lat_recv,
    par_send,
    par_recv,
    send_sem,
    recv_sem,
):
    tile = lax.axis_index("tile")
    chan = lax.axis_index("chan")
    mate = (tile, chan + 1 - 2 * lax.rem(chan, 2))
    far_chan = lax.rem(chan + 2, GROUPS)
    far = (tile, far_chan)
    core = lax.rem(chan, 2)
    here = 2 * core + chan // 2
    there = 2 * core + far_chan // 2
    both = pl.ds(2 * core, 2)
    mates = pl.ds(2 - 2 * core, 2)
    shifted = {d: lax.rem(tile + d + tiles, tiles) for d in (-2, -1, 1, 2)}
    right = (shifted[1], chan)
    left = (shifted[-1], chan)
    width = C // GROUPS
    total = tiles * span
    start = tile * span

    def remote(src, dst, send, recv, device):
        return pltpu.make_async_remote_copy(
            src_ref=src,
            dst_ref=dst,
            send_sem=send,
            recv_sem=recv,
            device_id=device,
            device_id_type=MESH,
        )

    barrier = pltpu.get_barrier_semaphore()
    near = {d: (tile + d >= 0) & (tile + d < tiles) for d in (-2, -1, 1, 2)}
    met = 2
    for d in (-1, 1):
        met = met + 2 * near[d].astype(jnp.int32)

        @pl.when(near[d])
        def _(d=d):
            for group in (chan, far_chan):
                device = (shifted[d], group)
                pl.semaphore_signal(barrier, inc=1, device_id=device, device_id_type=MESH)

    for device in (mate, far):
        pl.semaphore_signal(barrier, inc=1, device_id=device, device_id_type=MESH)

    local = [
        pltpu.make_async_copy(weight_a, wa, loc_sem.at[0]),
        pltpu.make_async_copy(weight_b, wb, loc_sem.at[1]),
        pltpu.make_async_copy(weight_up, wu, loc_sem.at[2]),
        pltpu.make_async_copy(cache_a, held_a.at[here], loc_sem.at[3]),
        pltpu.make_async_copy(cache_b, held_b.at[here], loc_sem.at[4]),
    ]
    fetched = (
        (latent_hbm, latent),
        (latent_cache_hbm, latent_cache),
        (weight_in_hbm, weight_in),
        (bias_in_hbm, bias_in),
        (gain_a_hbm, gain_a),
        (gain_b_hbm, gain_b),
        (bias_a_hbm, bias_a),
        (bias_b_hbm, bias_b),
        (bias_up_hbm, bias_up),
    )
    for number, (src, dst) in enumerate(fetched):
        local.append(pltpu.make_async_copy(src, dst, loc_sem.at[5 + number]))
    for number in (5, 6, 7, 3, 8, 9, 10, 11, 12, 13, 4, 0, 1, 2):
        local[number].start()

    def pack(which, buf, waited=None):
        if waited is not None:
            local[waited].wait()
        packs[which, 0], packs[which, 1] = rim_packs(buf[here, 0], buf[here, 1], span)

    for copy in local[5:]:
        copy.wait()
    own_lat[...] = jnp.concatenate(
        [latent_cache[0].astype(F32), latent_cache[1].astype(F32), latent[0].astype(F32), latent[1].astype(F32)],
        axis=0,
    ).astype(BF16)
    taps_first = jnp.concatenate(
        [weight_in[(a * 3 + b) * 3 + c].astype(F32) for b in range(3) for c in range(3) for a in range(3)],
        axis=0,
    )
    vectors = jnp.concatenate([bias_in[...], gain_a[...], gain_b[...]], axis=0)
    first = vectors.astype(BF16).astype(F32)
    second = (vectors - first).astype(BF16).astype(F32)
    third = (vectors - first - second).astype(BF16).astype(F32)
    rows = jnp.concatenate([taps_first, first, second, third, jnp.zeros((7, width), F32)], axis=0)
    win[here] = rows.T.astype(BF16)
    pack(0, held_a, 3)
    pl.semaphore_wait(barrier, met)

    sends = []

    def guarded(condition, act):
        if condition is None:
            act()
        else:
            pl.when(condition)(act)

    def go(copy, condition=None):
        guarded(condition, copy.start)
        sends.append((condition, copy))

    lat[here, 2] = own_lat[...]
    lat_waits = []
    for index, (d, group) in enumerate(((1, chan), (-1, chan), (1, far_chan), (-1, far_chan), (0, far_chan))):
        device = (shifted[d] if d else tile, group)
        copy = remote(own_lat, lat.at[here, 2 - d], lat_send.at[index], lat_recv.at[index], device)
        go(copy, near.get(d))
        lat_waits.append((near.get(-d), copy))
    go(remote(win.at[here], win.at[here], par_send.at[0], par_recv.at[0], far))

    def exchange_copy(which, src, dst, number, device):
        return remote(src, dst, send_sem.at[which, number], recv_sem.at[which, number], device)

    def send_own(which, own, rim):
        low = packs.at[which, 0]
        high = packs.at[which, 1]
        go(exchange_copy(which, low, rim.at[here, LOW], 4, (shifted[1], far_chan)), near[1])
        go(exchange_copy(which, high, rim.at[here, HIGH], 5, (shifted[-1], far_chan)), near[-1])
        go(exchange_copy(which, low, rim.at[here, LOW], 2, right), near[1])
        go(exchange_copy(which, high, rim.at[here, HIGH], 3, left), near[-1])
        go(exchange_copy(which, own.at[here], own.at[here], 1, far))

    def pass_on(which, own, rim):
        for numbers, onward, refs, ref in (
            ((1,), 6, (own.at[there],), own.at[both]),
            ((2, 3), 7, (rim.at[here, LOW], rim.at[here, HIGH]), rim.at[here]),
            ((4, 5), 8, (rim.at[there, LOW], rim.at[there, HIGH]), rim.at[there]),
        ):
            for number, landed in zip(numbers, refs):
                copy = exchange_copy(which, landed, landed, number, mate)
                guarded(None if number == 1 else near[1 if number % 2 else -1], copy.wait_recv)
            go(exchange_copy(which, ref, ref, onward, mate))

    def take_mate(which, own, rim):
        for number, ref in ((6, own.at[mates]), (7, rim.at[here]), (8, rim.at[there])):
            exchange_copy(which, ref, ref, number, mate).wait_recv()

    send_own(0, held_a, held_a_rim)

    between = near[-1] & near[1]
    for d in (1, -1):
        for number in ((0, 2) if d == 1 else (1, 3)):
            guarded(lat_waits[number][0], lat_waits[number][1].wait_recv)
        copy = remote(
            lat.at[both, 2 - d], lat.at[both, 2 - 2 * d], lat_send.at[5 + (d < 0)], lat_recv.at[5 + (d < 0)],
            (shifted[d], chan),
        )
        go(copy, between)
        lat_waits.append((near[-2 * d], copy))
    remote(win.at[here], win.at[there], par_send.at[0], par_recv.at[0], far).wait_recv()
    go(remote(win.at[both], win.at[both], par_send.at[1], par_recv.at[1], mate))
    for condition, copy in lat_waits[4:]:
        guarded(condition, copy.wait_recv)
    go(remote(lat.at[both], lat.at[both], lat_send.at[7], lat_recv.at[7], mate))
    pass_on(0, held_a, held_a_rim)
    pack(1, held_b, 4)
    send_own(1, held_b, held_b_rim)

    lane = lax.broadcasted_iota(jnp.int32, (1, LANES), 1)
    column = lax.rem(start + lane, W)
    inner_column = lax.rem(start + lane + (W - 1), W)
    first_column = column == 0
    last_column = column == W - 1

    def inside(step):
        cell = start + (step - 1) * W - 1 + lane
        return (cell >= 0) & (cell < total)

    remote(win.at[both], win.at[mates], par_send.at[1], par_recv.at[1], mate).wait_recv()
    order = (0, 2, 1, 3)
    depth = 27 * weight_in.shape[1]
    stem_left = jnp.concatenate([win[number] for number in order], axis=0)

    def full_column(number):
        parts = [stem_left[:, depth + number + 3 * k :][:, :1].astype(F32) for k in range(3)]
        return parts[0] + parts[1] + parts[2]

    bias_in_column = full_column(0)
    gain_a_column = full_column(1)
    gain_b_column = full_column(2)
    own_rows = jnp.concatenate([bias_a[...], bias_b[...], jnp.zeros((6, width), F32)], axis=0)
    par[...] = padded(own_rows, 128)
    par[2:3] = padded(bias_up[...], 128)
    own_columns = par[...].T
    bias_a_column = own_columns[:width, 0:1]
    bias_b_column = own_columns[:width, 1:2]
    bias_up_column = own_columns[: width // 2, 2:3]
    stem_left = stem_left[:, :depth]

    remote(lat.at[both], lat.at[mates], lat_send.at[7], lat_recv.at[7], mate).wait_recv()
    depth = GROUPS * own_lat.shape[0]
    place = lax.broadcasted_iota(jnp.int32, (depth, depth), 0)
    taken = lax.broadcasted_iota(jnp.int32, (depth, depth), 1)
    quarter = depth // 4
    small = quarter // GROUPS
    source = lax.rem(place, quarter) // small * quarter + place // quarter * small + lax.rem(place, small)
    sorter = jnp.where(source == taken, 1.0, 0.0).astype(BF16)
    wide = jnp.concatenate(
        [dot(sorter, jnp.concatenate([lat[number, d] for number in order], axis=0)) for d in range(5)], axis=1
    )
    cell = start - 2 * span + lax.broadcasted_iota(jnp.int32, (1, 5 * span), 1)
    wide = jnp.where((cell >= 0) & (cell < total), wide, 0.0)
    views = {}
    for row in range(5):
        for tap in range(3):
            begin = 2 * span + (row - 2) * W + tap - 2
            view = padded(wide[:, begin : begin + span + 2])
            if tap == 0:
                view = jnp.where(inner_column == 0, 0.0, view)
            if tap == 2:
                view = jnp.where(inner_column == W - 1, 0.0, view)
            views[row, tap] = view.astype(BF16)

    def activate(values, gain_column, step):
        values = values.astype(F32)
        scale = lax.rsqrt(jnp.sum(values * values, axis=0, keepdims=True) * (1.0 / C) + EPS)
        values = values * scale * gain_column
        values = values / (1.0 + jnp.exp(-values))
        return jnp.where(inside(step), values, 0.0).astype(BF16)

    for frame in range(2):
        for step in range(3):
            right_side = jnp.concatenate(
                [
                    views[step + b, c][frame * quarter : (frame + 3) * quarter]
                    for b in range(3)
                    for c in range(3)
                ],
                axis=0,
            )
            values = (dot(stem_left, right_side) + bias_in_column).astype(BF16)
            if step == 1:
                stem[frame] = values.reshape(GROUPS, C // GROUPS, LANES)
            maps[2 + frame, step] = activate(values, gain_a_column, step)

    def windows(own, rim, frame):
        low, high = (jnp.concatenate([rim[number, side] for number in order], axis=0) for side in (LOW, HIGH))
        middle = jnp.concatenate([own[number, frame] for number in order], axis=0)
        return row_windows(frame, low, middle, high, span)

    def load_windows(own, rim):
        for frame in range(2):
            for step, values in enumerate(windows(own, rim, frame)):
                maps[frame, step] = jnp.where(inside(step), values, jnp.zeros_like(values))

    def taps(weight, frame, time_taps):
        acc = None
        for a in time_taps:
            for b in range(3):
                term = dot(weight[a * 3 + b], maps[frame + a, b])
                acc = term if acc is None else acc + term
        return acc

    def finish(acc, frame, bias_column, added):
        middle = acc[width : 2 * width]
        if added is not None:
            middle = middle + added.astype(F32)
        result = jnp.where(first_column, 0.0, acc[:width])
        result = result + pltpu.roll(middle, LANES - 1, 1)
        result = result + jnp.where(last_column, 0.0, pltpu.roll(acc[2 * width :], LANES - 2, 1))
        return (result + bias_column).astype(BF16)[:, :span]

    local[0].wait()
    early[0] = taps(wa, 0, (2,))
    early[1] = taps(wa, 1, (1, 2))
    take_mate(0, held_a, held_a_rim)
    load_windows(held_a, held_a_rim)
    for frame in range(2):
        acc = early[frame] + taps(wa, frame, (0, 1) if frame == 0 else (0,))
        swap_a[here, frame] = finish(acc, frame, bias_a_column, None)
    pack(2, swap_a)
    send_own(2, swap_a, swap_a_rim)

    pass_on(1, held_b, held_b_rim)
    take_mate(1, held_b, held_b_rim)
    load_windows(held_b, held_b_rim)
    local[1].wait()
    early[0] = taps(wb, 0, (0, 1))
    early[1] = taps(wb, 1, (0,))

    pass_on(2, swap_a, swap_a_rim)
    take_mate(2, swap_a, swap_a_rim)
    for frame in range(2):
        for step, values in enumerate(windows(swap_a, swap_a_rim, frame)):
            maps[2 + frame, step] = activate(values, gain_b_column, step)
    for frame in range(2):
        acc = early[frame] + taps(wb, frame, (2,) if frame == 0 else (1, 2))
        swap_b[here, frame] = finish(acc, frame, bias_b_column, stem[frame, chan])
    pack(3, swap_b)
    send_own(3, swap_b, swap_b_rim)

    local[2].wait()
    outs = C // GROUPS // 2
    row_sets = (((0,), (1, 2)), ((0, 1), (2,)))
    column_sets = ((0,), (1, 2), (0, 1), (2,))
    for p in range(2):
        for half in range(2):
            for block in range(4):
                summed = None
                for b in row_sets[p][half]:
                    for c in column_sets[block]:
                        term = wu[b * 3 + c].astype(F32)
                        summed = term if summed is None else summed + term
                up_left[p, block * outs : (block + 1) * outs, half * C : (half + 1) * C] = summed.astype(
                    BF16
                )
    half_lanes = LANES // 2
    into = lax.broadcasted_iota(jnp.int32, (4 * half_lanes, 4 * half_lanes), 1)
    whence = lax.broadcasted_iota(jnp.int32, (4 * half_lanes, 4 * half_lanes), 0)
    wanted = lax.rem(whence, half_lanes) * 4 + whence // half_lanes
    spread[...] = jnp.where(into == wanted, 1.0, 0.0).astype(BF16)

    pass_on(3, swap_b, swap_b_rim)
    take_mate(3, swap_b, swap_b_rim)
    load_windows(swap_b, swap_b_rim)
    pieces = []
    for frame in range(2):
        quarters = []
        for p in range(2):
            acc = dot(up_left[p], maps[frame, p : p + 2].reshape(2 * C, LANES))
            even = jnp.where(first_column, 0.0, acc[:outs]) + pltpu.roll(acc[outs : 2 * outs], LANES - 1, 1)
            odd = pltpu.roll(acc[2 * outs : 3 * outs], LANES - 1, 1) + jnp.where(
                last_column, 0.0, pltpu.roll(acc[3 * outs :], LANES - 2, 1)
            )
            quarters += [(even + bias_up_column).astype(BF16), (odd + bias_up_column).astype(BF16)]
        pieces.append(quarters)
    for frame in range(2):
        quarters = pieces[frame]
        for side in range(2):
            joined = jnp.concatenate(
                [part[:, side * half_lanes : (side + 1) * half_lanes] for part in quarters], axis=1
            )
            woven = dot(joined, spread[...]).astype(BF16)
            first = side * 4 * half_lanes
            count = min(4 * half_lanes, 4 * span - first)
            out[frame, :, first : first + count] = woven[:, :count]

    for condition, copy in sends:
        guarded(condition, copy.wait_send)


def shards(tiles, *operands):
    (
        latent,
        latent_cache,
        weight_in,
        bias_in,
        cache_a,
        gain_a,
        weight_a,
        bias_a,
        cache_b,
        gain_b,
        weight_b,
        bias_b,
        weight_up,
        bias_up,
    ) = operands
    span = latent.shape[2]
    width = C // GROUPS
    small = latent.shape[1]
    depth = 27 * weight_in.shape[4]
    vmem = pl.BlockSpec(memory_space=pltpu.VMEM)
    hbm = pl.BlockSpec(memory_space=pl.ANY)
    block = pltpu.VMEM((GROUPS, 2, width, span), BF16)
    rim = pltpu.VMEM((GROUPS, 2, width, 384), BF16)
    dma = pltpu.SemaphoreType.DMA
    row = lambda vector: vector.reshape(1, -1)
    return pl.pallas_call(
        functools.partial(body, tiles, span),
        out_shape=jax.ShapeDtypeStruct((2, width // 2, 4 * span), BF16),
        in_specs=[hbm] * 14,
        out_specs=vmem,
        scratch_shapes=[
            pltpu.VMEM(latent.shape, BF16),
            pltpu.VMEM(latent.shape, BF16),
            pltpu.VMEM((27, weight_in.shape[4], width), BF16),
            *[pltpu.VMEM((1, width), F32)] * 5,
            pltpu.VMEM((1, width // 2), F32),
            pltpu.VMEM((4 * small, span), BF16),
            pltpu.VMEM((GROUPS, 5, 4 * small, span), BF16),
            pltpu.VMEM((GROUPS, width, depth + 16), BF16),
            pltpu.VMEM((8, 128), F32),
            block,
            rim,
            block,
            rim,
            block,
            rim,
            block,
            rim,
            pltpu.VMEM((4, 2, width, 384), BF16),
            pltpu.VMEM((2, GROUPS, width, LANES), BF16),
            pltpu.VMEM((4, 3, C, LANES), BF16),
            pltpu.VMEM((2, 3 * width, LANES), F32),
            pltpu.VMEM((9, 3 * width, C), BF16),
            pltpu.VMEM((9, 3 * width, C), BF16),
            pltpu.VMEM((9, width // 2, C), BF16),
            pltpu.VMEM((2, 4 * width // 2, 2 * C), BF16),
            pltpu.VMEM((2 * LANES, 2 * LANES), BF16),
            dma((14,)),
            dma((8,)),
            dma((8,)),
            dma((2,)),
            dma((2,)),
            dma((4, 9)),
            dma((4, 9)),
        ],
        compiler_params=pltpu.CompilerParams(
            collective_id=0, has_side_effects=True, vmem_limit_bytes=48 << 20
        ),
    )(
        *(pltpu.with_memory_space_constraint(operand, pltpu.HBM) for operand in (
        latent,
        latent_cache,
        weight_in.swapaxes(3, 4).reshape(27, -1, width),
        row(bias_in),
        cache_a,
        row(gain_a),
        weight_a.reshape(9, 3 * width, C),
        row(bias_a),
        cache_b,
        row(gain_b),
        weight_b.reshape(9, 3 * width, C),
        row(bias_b),
        weight_up.reshape(9, width // 2, C),
        row(bias_up),
    )))


def solution(mesh):
    placed = (
        P(None, "chan", "tile"),
        P(None, "chan", "tile"),
        P(None, None, None, "chan", None),
        P("chan"),
        P(None, "chan", "tile"),
        P("chan"),
        P(None, None, None, "chan", None),
        P("chan"),
        P(None, "chan", "tile"),
        P("chan"),
        P(None, None, None, "chan", None),
        P("chan"),
        P(None, None, "chan", None),
        P("chan"),
    )
    return jax.shard_map(
        functools.partial(shards, mesh.shape["tile"]),
        mesh=mesh,
        in_specs=placed,
        out_specs=P(None, "chan", "tile"),
        check_vma=False,
    )
```

```python
import functools

import jax
import jax.numpy as jnp
from jax import lax
from jax.experimental import pallas as pl
from jax.experimental.pallas import tpu as pltpu
from jax.sharding import PartitionSpec as P

C = 384
W = 160
EPS = 1e-06
LANES = 256
GROUPS = 4
MESH = pl.DeviceIdType.MESH
LOW, HIGH = 0, 1
F32 = jnp.float32
BF16 = jnp.bfloat16


def dot(a, b):
    return lax.dot_general(a, b, (((1,), (0,)), ((), ())), preferred_element_type=F32)


def padded(value, lanes=LANES):
    rows, count = value.shape
    return jnp.concatenate([value, jnp.zeros((rows, lanes - count), value.dtype)], axis=1)


def rim_packs(first, second, span):
    zeros = lambda count: jnp.zeros((first.shape[0], count), first.dtype)
    last = span - W - 1
    rest = W + 1 - 128
    low = jnp.concatenate(
        [
            first[:, last : last + 128],
            second[:, last : last + 128],
            first[:, span - rest :],
            zeros(64 - rest),
            second[:, span - rest :],
            zeros(64 - rest),
        ],
        axis=1,
    )
    head = 128 - (span - W + 1)
    tail = W + 1 - head
    high = jnp.concatenate(
        [
            first[:, head : W + 1],
            zeros(128 - tail),
            second[:, head : W + 1],
            zeros(128 - tail),
            zeros(64 - head),
            second[:, :head],
            zeros(64 - head),
            first[:, :head],
        ],
        axis=1,
    )
    return low, high


def row_windows(frame, low, own, high, span):
    zeros = jnp.zeros((own.shape[0], LANES - span - 2), own.dtype)
    rest = W + 1 - 128
    head = 128 - (span - W + 1)
    tail = W + 1 - head
    at_low = 256 + 64 * frame
    at_high = 256 + 64 * (2 - frame) - head
    return (
        jnp.concatenate(
            [
                low[:, 128 * frame : 128 * frame + 128],
                low[:, at_low : at_low + rest],
                own[:, : span + 1 - W],
                zeros,
            ],
            axis=1,
        ),
        jnp.concatenate(
            [low[:, at_low + rest - 1 : at_low + rest], own, high[:, at_high : at_high + 1], zeros], axis=1
        ),
        jnp.concatenate(
            [
                own[:, W - 1 :],
                high[:, at_high : at_high + head],
                high[:, 128 * frame : 128 * frame + tail],
                zeros,
            ],
            axis=1,
        ),
    )


def body(
    tiles,
    span,
    latent_hbm,
    latent_cache_hbm,
    weight_in_hbm,
    bias_in_hbm,
    cache_a,
    gain_a_hbm,
    weight_a,
    bias_a_hbm,
    cache_b,
    gain_b_hbm,
    weight_b,
    bias_b_hbm,
    weight_up,
    bias_up_hbm,
    out,
    latent,
    latent_cache,
    weight_in,
    bias_in,
    gain_a,
    bias_a,
    gain_b,
    bias_b,
    bias_up,
    own_lat,
    lat,
    win,
    par,
    held_a,
    held_a_rim,
    held_b,
    held_b_rim,
    swap_a,
    swap_a_rim,
    swap_b,
    swap_b_rim,
    packs,
    stem,
    maps,
    early,
    wa,
    wb,
    wu,
    up_left,
    spread,
    loc_sem,
    lat_send,
    lat_recv,
    par_send,
    par_recv,
    send_sem,
    recv_sem,
):
    tile = lax.axis_index("tile")
    chan = lax.axis_index("chan")
    mate = (tile, chan + 1 - 2 * lax.rem(chan, 2))
    far_chan = lax.rem(chan + 2, GROUPS)
    far = (tile, far_chan)
    core = lax.rem(chan, 2)
    here = 2 * core + chan // 2
    there = 2 * core + far_chan // 2
    both = pl.ds(2 * core, 2)
    mates = pl.ds(2 - 2 * core, 2)
    shifted = {d: lax.rem(tile + d + tiles, tiles) for d in (-2, -1, 1, 2)}
    right = (shifted[1], chan)
    left = (shifted[-1], chan)
    width = C // GROUPS
    total = tiles * span
    start = tile * span

    def remote(src, dst, send, recv, device):
        return pltpu.make_async_remote_copy(
            src_ref=src,
            dst_ref=dst,
            send_sem=send,
            recv_sem=recv,
            device_id=device,
            device_id_type=MESH,
        )

    barrier = pltpu.get_barrier_semaphore()
    near = {d: (tile + d >= 0) & (tile + d < tiles) for d in (-2, -1, 1, 2)}
    met = 2
    for d in (-1, 1):
        met = met + 2 * near[d].astype(jnp.int32)

        @pl.when(near[d])
        def _(d=d):
            for group in (chan, far_chan):
                device = (shifted[d], group)
                pl.semaphore_signal(barrier, inc=1, device_id=device, device_id_type=MESH)

    for device in (mate, far):
        pl.semaphore_signal(barrier, inc=1, device_id=device, device_id_type=MESH)

    local = [
        pltpu.make_async_copy(weight_a, wa, loc_sem.at[0]),
        pltpu.make_async_copy(weight_b, wb, loc_sem.at[1]),
        pltpu.make_async_copy(weight_up, wu, loc_sem.at[2]),
        pltpu.make_async_copy(cache_a, held_a.at[here], loc_sem.at[3]),
        pltpu.make_async_copy(cache_b, held_b.at[here], loc_sem.at[4]),
    ]
    fetched = (
        (latent_hbm, latent),
        (latent_cache_hbm, latent_cache),
        (weight_in_hbm, weight_in),
        (bias_in_hbm, bias_in),
        (gain_a_hbm, gain_a),
        (gain_b_hbm, gain_b),
        (bias_a_hbm, bias_a),
        (bias_b_hbm, bias_b),
        (bias_up_hbm, bias_up),
    )
    for number, (src, dst) in enumerate(fetched):
        local.append(pltpu.make_async_copy(src, dst, loc_sem.at[5 + number]))
    for number in (5, 6, 7, 3, 8, 9, 10, 11, 12, 13, 4, 0, 1, 2):
        local[number].start()

    def pack(which, buf, waited=None):
        if waited is not None:
            local[waited].wait()
        packs[which, 0], packs[which, 1] = rim_packs(buf[here, 0], buf[here, 1], span)

    for copy in local[5:]:
        copy.wait()
    own_lat[...] = jnp.concatenate(
        [latent_cache[0].astype(F32), latent_cache[1].astype(F32), latent[0].astype(F32), latent[1].astype(F32)],
        axis=0,
    ).astype(BF16)
    taps_first = jnp.concatenate(
        [weight_in[(a * 3 + b) * 3 + c].astype(F32) for b in range(3) for c in range(3) for a in range(3)],
        axis=0,
    )
    vectors = jnp.concatenate([bias_in[...], gain_a[...], gain_b[...]], axis=0)
    first = vectors.astype(BF16).astype(F32)
    second = (vectors - first).astype(BF16).astype(F32)
    third = (vectors - first - second).astype(BF16).astype(F32)
    rows = jnp.concatenate([taps_first, first, second, third, jnp.zeros((7, width), F32)], axis=0)
    win[here] = rows.T.astype(BF16)
    pack(0, held_a, 3)
    pl.semaphore_wait(barrier, met)

    sends = []

    def guarded(condition, act):
        if condition is None:
            act()
        else:
            pl.when(condition)(act)

    def go(copy, condition=None):
        guarded(condition, copy.start)
        sends.append((condition, copy))

    lat[here, 2] = own_lat[...]
    lat_waits = []
    for index, (d, group) in enumerate(((1, chan), (-1, chan), (1, far_chan), (-1, far_chan), (0, far_chan))):
        device = (shifted[d] if d else tile, group)
        copy = remote(own_lat, lat.at[here, 2 - d], lat_send.at[index], lat_recv.at[index], device)
        go(copy, near.get(d))
        lat_waits.append((near.get(-d), copy))
    go(remote(win.at[here], win.at[here], par_send.at[0], par_recv.at[0], far))

    def exchange_copy(which, src, dst, number, device):
        return remote(src, dst, send_sem.at[which, number], recv_sem.at[which, number], device)

    def send_own(which, own, rim):
        low = packs.at[which, 0]
        high = packs.at[which, 1]
        go(exchange_copy(which, low, rim.at[here, LOW], 4, (shifted[1], far_chan)), near[1])
        go(exchange_copy(which, high, rim.at[here, HIGH], 5, (shifted[-1], far_chan)), near[-1])
        go(exchange_copy(which, low, rim.at[here, LOW], 2, right), near[1])
        go(exchange_copy(which, high, rim.at[here, HIGH], 3, left), near[-1])
        go(exchange_copy(which, own.at[here], own.at[here], 1, far))

    def pass_on(which, own, rim):
        for numbers, onward, refs, ref in (
            ((1,), 6, (own.at[there],), own.at[both]),
            ((2, 3), 7, (rim.at[here, LOW], rim.at[here, HIGH]), rim.at[here]),
            ((4, 5), 8, (rim.at[there, LOW], rim.at[there, HIGH]), rim.at[there]),
        ):
            for number, landed in zip(numbers, refs):
                copy = exchange_copy(which, landed, landed, number, mate)
                guarded(None if number == 1 else near[1 if number % 2 else -1], copy.wait_recv)
            go(exchange_copy(which, ref, ref, onward, mate))

    def take_mate(which, own, rim):
        for number, ref in ((6, own.at[mates]), (7, rim.at[here]), (8, rim.at[there])):
            exchange_copy(which, ref, ref, number, mate).wait_recv()

    send_own(0, held_a, held_a_rim)

    between = near[-1] & near[1]
    for d in (1, -1):
        for number in ((0, 2) if d == 1 else (1, 3)):
            guarded(lat_waits[number][0], lat_waits[number][1].wait_recv)
        copy = remote(
            lat.at[both, 2 - d], lat.at[both, 2 - 2 * d], lat_send.at[5 + (d < 0)], lat_recv.at[5 + (d < 0)],
            (shifted[d], chan),
        )
        go(copy, between)
        lat_waits.append((near[-2 * d], copy))
    remote(win.at[here], win.at[there], par_send.at[0], par_recv.at[0], far).wait_recv()
    go(remote(win.at[both], win.at[both], par_send.at[1], par_recv.at[1], mate))
    for condition, copy in lat_waits[4:]:
        guarded(condition, copy.wait_recv)
    go(remote(lat.at[both], lat.at[both], lat_send.at[7], lat_recv.at[7], mate))
    pass_on(0, held_a, held_a_rim)
    pack(1, held_b, 4)
    send_own(1, held_b, held_b_rim)

    lane = lax.broadcasted_iota(jnp.int32, (1, LANES), 1)
    column = lax.rem(start + lane, W)
    inner_column = lax.rem(start + lane + (W - 1), W)
    first_column = column == 0
    last_column = column == W - 1

    def inside(step):
        cell = start + (step - 1) * W - 1 + lane
        return (cell >= 0) & (cell < total)

    remote(win.at[both], win.at[mates], par_send.at[1], par_recv.at[1], mate).wait_recv()
    order = (0, 2, 1, 3)
    depth = 27 * weight_in.shape[1]
    stem_left = jnp.concatenate([win[number] for number in order], axis=0)

    def full_column(number):
        parts = [stem_left[:, depth + number + 3 * k :][:, :1].astype(F32) for k in range(3)]
        return parts[0] + parts[1] + parts[2]

    bias_in_column = full_column(0)
    gain_a_column = full_column(1)
    gain_b_column = full_column(2)
    own_rows = jnp.concatenate([bias_a[...], bias_b[...], jnp.zeros((6, width), F32)], axis=0)
    par[...] = padded(own_rows, 128)
    par[2:3] = padded(bias_up[...], 128)
    own_columns = par[...].T
    bias_a_column = own_columns[:width, 0:1]
    bias_b_column = own_columns[:width, 1:2]
    bias_up_column = own_columns[: width // 2, 2:3]
    stem_left = stem_left[:, :depth]

    remote(lat.at[both], lat.at[mates], lat_send.at[7], lat_recv.at[7], mate).wait_recv()
    depth = GROUPS * own_lat.shape[0]
    place = lax.broadcasted_iota(jnp.int32, (depth, depth), 0)
    taken = lax.broadcasted_iota(jnp.int32, (depth, depth), 1)
    quarter = depth // 4
    small = quarter // GROUPS
    source = lax.rem(place, quarter) // small * quarter + place // quarter * small + lax.rem(place, small)
    sorter = jnp.where(source == taken, 1.0, 0.0).astype(BF16)
    wide = jnp.concatenate(
        [dot(sorter, jnp.concatenate([lat[number, d] for number in order], axis=0)) for d in range(5)], axis=1
    )
    cell = start - 2 * span + lax.broadcasted_iota(jnp.int32, (1, 5 * span), 1)
    wide = jnp.where((cell >= 0) & (cell < total), wide, 0.0)
    views = {}
    for row in range(5):
        for tap in range(3):
            begin = 2 * span + (row - 2) * W + tap - 2
            view = padded(wide[:, begin : begin + span + 2])
            if tap == 0:
                view = jnp.where(inner_column == 0, 0.0, view)
            if tap == 2:
                view = jnp.where(inner_column == W - 1, 0.0, view)
            views[row, tap] = view.astype(BF16)

    def activate(values, gain_column, step):
        values = values.astype(F32)
        scale = lax.rsqrt(jnp.sum(values * values, axis=0, keepdims=True) * (1.0 / C) + EPS)
        values = values * scale * gain_column
        values = values / (1.0 + jnp.exp(-values))
        return jnp.where(inside(step), values, 0.0).astype(BF16)

    for frame in range(2):
        for step in range(3):
            right_side = jnp.concatenate(
                [
                    views[step + b, c][frame * quarter : (frame + 3) * quarter]
                    for b in range(3)
                    for c in range(3)
                ],
                axis=0,
            )
            values = (dot(stem_left, right_side) + bias_in_column).astype(BF16)
            if step == 1:
                stem[frame] = values.reshape(GROUPS, C // GROUPS, LANES)
            maps[2 + frame, step] = activate(values, gain_a_column, step)

    def windows(own, rim, frame):
        low, high = (jnp.concatenate([rim[number, side] for number in order], axis=0) for side in (LOW, HIGH))
        middle = jnp.concatenate([own[number, frame] for number in order], axis=0)
        return row_windows(frame, low, middle, high, span)

    def load_windows(own, rim):
        for frame in range(2):
            for step, values in enumerate(windows(own, rim, frame)):
                maps[frame, step] = jnp.where(inside(step), values, jnp.zeros_like(values))

    def taps(weight, frame, time_taps):
        acc = None
        for a in time_taps:
            rows = jnp.concatenate([weight[a * 3 + b] for b in range(3)], axis=1)
            term = dot(rows, maps[frame + a].reshape(3 * C, LANES))
            acc = term if acc is None else acc + term
        return acc

    def finish(acc, frame, bias_column, added):
        middle = acc[width : 2 * width]
        if added is not None:
            middle = middle + added.astype(F32)
        result = jnp.where(first_column, 0.0, acc[:width])
        result = result + pltpu.roll(middle, LANES - 1, 1)
        result = result + jnp.where(last_column, 0.0, pltpu.roll(acc[2 * width :], LANES - 2, 1))
        return (result + bias_column).astype(BF16)[:, :span]

    local[0].wait()
    early[0] = taps(wa, 0, (2,))
    early[1] = taps(wa, 1, (1, 2))
    take_mate(0, held_a, held_a_rim)
    load_windows(held_a, held_a_rim)
    for frame in range(2):
        acc = early[frame] + taps(wa, frame, (0, 1) if frame == 0 else (0,))
        swap_a[here, frame] = finish(acc, frame, bias_a_column, None)
    pack(2, swap_a)
    send_own(2, swap_a, swap_a_rim)

    pass_on(1, held_b, held_b_rim)
    take_mate(1, held_b, held_b_rim)
    load_windows(held_b, held_b_rim)
    local[1].wait()
    early[0] = taps(wb, 0, (0, 1))
    early[1] = taps(wb, 1, (0,))

    pass_on(2, swap_a, swap_a_rim)
    take_mate(2, swap_a, swap_a_rim)
    for frame in range(2):
        for step, values in enumerate(windows(swap_a, swap_a_rim, frame)):
            maps[2 + frame, step] = activate(values, gain_b_column, step)
    for frame in range(2):
        acc = early[frame] + taps(wb, frame, (2,) if frame == 0 else (1, 2))
        swap_b[here, frame] = finish(acc, frame, bias_b_column, stem[frame, chan])
    pack(3, swap_b)
    send_own(3, swap_b, swap_b_rim)

    local[2].wait()
    outs = C // GROUPS // 2
    row_sets = (((0,), (1, 2)), ((0, 1), (2,)))
    column_sets = ((0,), (1, 2), (0, 1), (2,))
    for p in range(2):
        for half in range(2):
            for block in range(4):
                summed = None
                for b in row_sets[p][half]:
                    for c in column_sets[block]:
                        term = wu[b * 3 + c].astype(F32)
                        summed = term if summed is None else summed + term
                up_left[p, block * outs : (block + 1) * outs, half * C : (half + 1) * C] = summed.astype(
                    BF16
                )
    half_lanes = LANES // 2
    into = lax.broadcasted_iota(jnp.int32, (4 * half_lanes, 4 * half_lanes), 1)
    whence = lax.broadcasted_iota(jnp.int32, (4 * half_lanes, 4 * half_lanes), 0)
    wanted = lax.rem(whence, half_lanes) * 4 + whence // half_lanes
    spread[...] = jnp.where(into == wanted, 1.0, 0.0).astype(BF16)

    pass_on(3, swap_b, swap_b_rim)
    take_mate(3, swap_b, swap_b_rim)
    load_windows(swap_b, swap_b_rim)
    pieces = []
    for frame in range(2):
        quarters = []
        for p in range(2):
            acc = dot(up_left[p], maps[frame, p : p + 2].reshape(2 * C, LANES))
            even = jnp.where(first_column, 0.0, acc[:outs]) + pltpu.roll(acc[outs : 2 * outs], LANES - 1, 1)
            odd = pltpu.roll(acc[2 * outs : 3 * outs], LANES - 1, 1) + jnp.where(
                last_column, 0.0, pltpu.roll(acc[3 * outs :], LANES - 2, 1)
            )
            quarters += [(even + bias_up_column).astype(BF16), (odd + bias_up_column).astype(BF16)]
        pieces.append(quarters)
    for frame in range(2):
        quarters = pieces[frame]
        for side in range(2):
            joined = jnp.concatenate(
                [part[:, side * half_lanes : (side + 1) * half_lanes] for part in quarters], axis=1
            )
            woven = dot(joined, spread[...]).astype(BF16)
            first = side * 4 * half_lanes
            count = min(4 * half_lanes, 4 * span - first)
            out[frame, :, first : first + count] = woven[:, :count]

    for condition, copy in sends:
        guarded(condition, copy.wait_send)


def shards(tiles, *operands):
    (
        latent,
        latent_cache,
        weight_in,
        bias_in,
        cache_a,
        gain_a,
        weight_a,
        bias_a,
        cache_b,
        gain_b,
        weight_b,
        bias_b,
        weight_up,
        bias_up,
    ) = operands
    span = latent.shape[2]
    width = C // GROUPS
    small = latent.shape[1]
    depth = 27 * weight_in.shape[4]
    vmem = pl.BlockSpec(memory_space=pltpu.VMEM)
    hbm = pl.BlockSpec(memory_space=pl.ANY)
    block = pltpu.VMEM((GROUPS, 2, width, span), BF16)
    rim = pltpu.VMEM((GROUPS, 2, width, 384), BF16)
    dma = pltpu.SemaphoreType.DMA
    row = lambda vector: vector.reshape(1, -1)
    return pl.pallas_call(
        functools.partial(body, tiles, span),
        out_shape=jax.ShapeDtypeStruct((2, width // 2, 4 * span), BF16),
        in_specs=[hbm] * 14,
        out_specs=vmem,
        scratch_shapes=[
            pltpu.VMEM(latent.shape, BF16),
            pltpu.VMEM(latent.shape, BF16),
            pltpu.VMEM((27, weight_in.shape[4], width), BF16),
            *[pltpu.VMEM((1, width), F32)] * 5,
            pltpu.VMEM((1, width // 2), F32),
            pltpu.VMEM((4 * small, span), BF16),
            pltpu.VMEM((GROUPS, 5, 4 * small, span), BF16),
            pltpu.VMEM((GROUPS, width, depth + 16), BF16),
            pltpu.VMEM((8, 128), F32),
            block,
            rim,
            block,
            rim,
            block,
            rim,
            block,
            rim,
            pltpu.VMEM((4, 2, width, 384), BF16),
            pltpu.VMEM((2, GROUPS, width, LANES), BF16),
            pltpu.VMEM((4, 3, C, LANES), BF16),
            pltpu.VMEM((2, 3 * width, LANES), F32),
            pltpu.VMEM((9, 3 * width, C), BF16),
            pltpu.VMEM((9, 3 * width, C), BF16),
            pltpu.VMEM((9, width // 2, C), BF16),
            pltpu.VMEM((2, 4 * width // 2, 2 * C), BF16),
            pltpu.VMEM((2 * LANES, 2 * LANES), BF16),
            dma((14,)),
            dma((8,)),
            dma((8,)),
            dma((2,)),
            dma((2,)),
            dma((4, 9)),
            dma((4, 9)),
        ],
        compiler_params=pltpu.CompilerParams(
            collective_id=0, has_side_effects=True, vmem_limit_bytes=48 << 20
        ),
    )(
        *(pltpu.with_memory_space_constraint(operand, pltpu.HBM) for operand in (
        latent,
        latent_cache,
        weight_in.swapaxes(3, 4).reshape(27, -1, width),
        row(bias_in),
        cache_a,
        row(gain_a),
        weight_a.reshape(9, 3 * width, C),
        row(bias_a),
        cache_b,
        row(gain_b),
        weight_b.reshape(9, 3 * width, C),
        row(bias_b),
        weight_up.reshape(9, width // 2, C),
        row(bias_up),
    )))


def solution(mesh):
    placed = (
        P(None, "chan", "tile"),
        P(None, "chan", "tile"),
        P(None, None, None, "chan", None),
        P("chan"),
        P(None, "chan", "tile"),
        P("chan"),
        P(None, None, None, "chan", None),
        P("chan"),
        P(None, "chan", "tile"),
        P("chan"),
        P(None, None, None, "chan", None),
        P("chan"),
        P(None, None, "chan", None),
        P("chan"),
    )
    return jax.shard_map(
        functools.partial(shards, mesh.shape["tile"]),
        mesh=mesh,
        in_specs=placed,
        out_specs=P(None, "chan", "tile"),
        check_vma=False,
    )
```

```python
import functools

import jax
import jax.numpy as jnp
from jax import lax
from jax.experimental import pallas as pl
from jax.experimental.pallas import tpu as pltpu
from jax.sharding import PartitionSpec as P

C = 384
W = 160
EPS = 1e-06
LANES = 256
GROUPS = 4
MESH = pl.DeviceIdType.MESH
LOW, HIGH = 0, 1
F32 = jnp.float32
BF16 = jnp.bfloat16


def dot(a, b):
    return lax.dot_general(a, b, (((1,), (0,)), ((), ())), preferred_element_type=F32)


def padded(value, lanes=LANES):
    rows, count = value.shape
    return jnp.concatenate([value, jnp.zeros((rows, lanes - count), value.dtype)], axis=1)


def rim_packs(first, second, span):
    zeros = lambda count: jnp.zeros((first.shape[0], count), first.dtype)
    last = span - W - 1
    rest = W + 1 - 128
    low = jnp.concatenate(
        [
            first[:, last : last + 128],
            second[:, last : last + 128],
            first[:, span - rest :],
            zeros(64 - rest),
            second[:, span - rest :],
            zeros(64 - rest),
        ],
        axis=1,
    )
    head = 128 - (span - W + 1)
    tail = W + 1 - head
    high = jnp.concatenate(
        [
            first[:, head : W + 1],
            zeros(128 - tail),
            second[:, head : W + 1],
            zeros(128 - tail),
            zeros(64 - head),
            second[:, :head],
            zeros(64 - head),
            first[:, :head],
        ],
        axis=1,
    )
    return low, high


def row_windows(frame, low, own, high, span):
    zeros = jnp.zeros((own.shape[0], LANES - span - 2), own.dtype)
    rest = W + 1 - 128
    head = 128 - (span - W + 1)
    tail = W + 1 - head
    at_low = 256 + 64 * frame
    at_high = 256 + 64 * (2 - frame) - head
    return (
        jnp.concatenate(
            [
                low[:, 128 * frame : 128 * frame + 128],
                low[:, at_low : at_low + rest],
                own[:, : span + 1 - W],
                zeros,
            ],
            axis=1,
        ),
        jnp.concatenate(
            [low[:, at_low + rest - 1 : at_low + rest], own, high[:, at_high : at_high + 1], zeros], axis=1
        ),
        jnp.concatenate(
            [
                own[:, W - 1 :],
                high[:, at_high : at_high + head],
                high[:, 128 * frame : 128 * frame + tail],
                zeros,
            ],
            axis=1,
        ),
    )


def body(
    tiles,
    span,
    latent_hbm,
    latent_cache_hbm,
    weight_in_hbm,
    bias_in_hbm,
    cache_a,
    gain_a_hbm,
    weight_a,
    bias_a_hbm,
    cache_b,
    gain_b_hbm,
    weight_b,
    bias_b_hbm,
    weight_up,
    bias_up_hbm,
    out,
    latent,
    latent_cache,
    weight_in,
    bias_in,
    gain_a,
    bias_a,
    gain_b,
    bias_b,
    bias_up,
    own_lat,
    lat,
    win,
    par,
    held_a,
    held_a_rim,
    held_b,
    held_b_rim,
    swap_a,
    swap_a_rim,
    swap_b,
    swap_b_rim,
    packs,
    stem,
    maps,
    early,
    wa,
    wb,
    wu,
    up_left,
    spread,
    loc_sem,
    lat_send,
    lat_recv,
    par_send,
    par_recv,
    send_sem,
    recv_sem,
):
    tile = lax.axis_index("tile")
    chan = lax.axis_index("chan")
    mate = (tile, chan + 1 - 2 * lax.rem(chan, 2))
    far_chan = lax.rem(chan + 2, GROUPS)
    far = (tile, far_chan)
    core = lax.rem(chan, 2)
    here = 2 * core + chan // 2
    there = 2 * core + far_chan // 2
    both = pl.ds(2 * core, 2)
    mates = pl.ds(2 - 2 * core, 2)
    shifted = {d: lax.rem(tile + d + tiles, tiles) for d in (-2, -1, 1, 2)}
    right = (shifted[1], chan)
    left = (shifted[-1], chan)
    width = C // GROUPS
    total = tiles * span
    start = tile * span

    def remote(src, dst, send, recv, device):
        return pltpu.make_async_remote_copy(
            src_ref=src,
            dst_ref=dst,
            send_sem=send,
            recv_sem=recv,
            device_id=device,
            device_id_type=MESH,
        )

    barrier = pltpu.get_barrier_semaphore()
    near = {d: (tile + d >= 0) & (tile + d < tiles) for d in (-2, -1, 1, 2)}
    met = 2
    for d in (-1, 1):
        met = met + 2 * near[d].astype(jnp.int32)

        @pl.when(near[d])
        def _(d=d):
            for group in (chan, far_chan):
                device = (shifted[d], group)
                pl.semaphore_signal(barrier, inc=1, device_id=device, device_id_type=MESH)

    for device in (mate, far):
        pl.semaphore_signal(barrier, inc=1, device_id=device, device_id_type=MESH)

    local = [
        pltpu.make_async_copy(weight_a, wa, loc_sem.at[0]),
        pltpu.make_async_copy(weight_b, wb, loc_sem.at[1]),
        pltpu.make_async_copy(weight_up, wu, loc_sem.at[2]),
        pltpu.make_async_copy(cache_a, held_a.at[here], loc_sem.at[3]),
        pltpu.make_async_copy(cache_b, held_b.at[here], loc_sem.at[4]),
    ]
    fetched = (
        (latent_hbm, latent),
        (latent_cache_hbm, latent_cache),
        (weight_in_hbm, weight_in),
        (bias_in_hbm, bias_in),
        (gain_a_hbm, gain_a),
        (gain_b_hbm, gain_b),
        (bias_a_hbm, bias_a),
        (bias_b_hbm, bias_b),
        (bias_up_hbm, bias_up),
    )
    for number, (src, dst) in enumerate(fetched):
        local.append(pltpu.make_async_copy(src, dst, loc_sem.at[5 + number]))
    for number in (5, 6, 7, 3, 8, 9, 10, 11, 12, 13, 4, 0, 1, 2):
        local[number].start()

    def pack(which, buf, waited=None):
        if waited is not None:
            local[waited].wait()
        packs[which, 0], packs[which, 1] = rim_packs(buf[here, 0], buf[here, 1], span)

    for copy in local[5:]:
        copy.wait()
    own_lat[...] = jnp.concatenate(
        [latent_cache[0].astype(F32), latent_cache[1].astype(F32), latent[0].astype(F32), latent[1].astype(F32)],
        axis=0,
    ).astype(BF16)
    taps_first = jnp.concatenate(
        [weight_in[(a * 3 + b) * 3 + c].astype(F32) for b in range(3) for c in range(3) for a in range(3)],
        axis=0,
    )
    vectors = jnp.concatenate([bias_in[...], gain_a[...], gain_b[...]], axis=0)
    first = vectors.astype(BF16).astype(F32)
    second = (vectors - first).astype(BF16).astype(F32)
    third = (vectors - first - second).astype(BF16).astype(F32)
    rows = jnp.concatenate([taps_first, first, second, third, jnp.zeros((7, width), F32)], axis=0)
    win[here] = rows.T.astype(BF16)
    pack(0, held_a, 3)
    pl.semaphore_wait(barrier, met)

    sends = []

    def guarded(condition, act):
        if condition is None:
            act()
        else:
            pl.when(condition)(act)

    def go(copy, condition=None):
        guarded(condition, copy.start)
        sends.append((condition, copy))

    go(remote(win.at[here], win.at[here], par_send.at[0], par_recv.at[0], far))
    lat[here, 2] = own_lat[...]
    lat_waits = []
    for index, (d, group) in enumerate(((1, chan), (-1, chan), (1, far_chan), (-1, far_chan), (0, far_chan))):
        device = (shifted[d] if d else tile, group)
        copy = remote(own_lat, lat.at[here, 2 - d], lat_send.at[index], lat_recv.at[index], device)
        go(copy, near.get(d))
        lat_waits.append((near.get(-d), copy))

    def exchange_copy(which, src, dst, number, device):
        return remote(src, dst, send_sem.at[which, number], recv_sem.at[which, number], device)

    def send_own(which, own, rim):
        low = packs.at[which, 0]
        high = packs.at[which, 1]
        go(exchange_copy(which, low, rim.at[here, LOW], 4, (shifted[1], far_chan)), near[1])
        go(exchange_copy(which, high, rim.at[here, HIGH], 5, (shifted[-1], far_chan)), near[-1])
        go(exchange_copy(which, low, rim.at[here, LOW], 2, right), near[1])
        go(exchange_copy(which, high, rim.at[here, HIGH], 3, left), near[-1])
        go(exchange_copy(which, own.at[here], own.at[here], 1, far))

    def pass_on(which, own, rim):
        for numbers, onward, refs, ref in (
            ((1,), 6, (own.at[there],), own.at[both]),
            ((2, 3), 7, (rim.at[here, LOW], rim.at[here, HIGH]), rim.at[here]),
            ((4, 5), 8, (rim.at[there, LOW], rim.at[there, HIGH]), rim.at[there]),
        ):
            for number, landed in zip(numbers, refs):
                copy = exchange_copy(which, landed, landed, number, mate)
                guarded(None if number == 1 else near[1 if number % 2 else -1], copy.wait_recv)
            go(exchange_copy(which, ref, ref, onward, mate))

    def take_mate(which, own, rim):
        for number, ref in ((6, own.at[mates]), (7, rim.at[here]), (8, rim.at[there])):
            exchange_copy(which, ref, ref, number, mate).wait_recv()

    send_own(0, held_a, held_a_rim)

    between = near[-1] & near[1]
    for d in (1, -1):
        for number in ((0, 2) if d == 1 else (1, 3)):
            guarded(lat_waits[number][0], lat_waits[number][1].wait_recv)
        copy = remote(
            lat.at[both, 2 - d], lat.at[both, 2 - 2 * d], lat_send.at[5 + (d < 0)], lat_recv.at[5 + (d < 0)],
            (shifted[d], chan),
        )
        go(copy, between)
        lat_waits.append((near[-2 * d], copy))
    remote(win.at[here], win.at[there], par_send.at[0], par_recv.at[0], far).wait_recv()
    go(remote(win.at[both], win.at[both], par_send.at[1], par_recv.at[1], mate))
    for condition, copy in lat_waits[4:]:
        guarded(condition, copy.wait_recv)
    go(remote(lat.at[both], lat.at[both], lat_send.at[7], lat_recv.at[7], mate))
    pass_on(0, held_a, held_a_rim)
    pack(1, held_b, 4)
    send_own(1, held_b, held_b_rim)

    lane = lax.broadcasted_iota(jnp.int32, (1, LANES), 1)
    column = lax.rem(start + lane, W)
    inner_column = lax.rem(start + lane + (W - 1), W)
    first_column = column == 0
    last_column = column == W - 1

    def inside(step):
        cell = start + (step - 1) * W - 1 + lane
        return (cell >= 0) & (cell < total)

    remote(win.at[both], win.at[mates], par_send.at[1], par_recv.at[1], mate).wait_recv()
    order = (0, 2, 1, 3)
    depth = 27 * weight_in.shape[1]
    stem_left = jnp.concatenate([win[number] for number in order], axis=0)

    def full_column(number):
        parts = [stem_left[:, depth + number + 3 * k :][:, :1].astype(F32) for k in range(3)]
        return parts[0] + parts[1] + parts[2]

    bias_in_column = full_column(0)
    gain_a_column = full_column(1)
    gain_b_column = full_column(2)
    own_rows = jnp.concatenate([bias_a[...], bias_b[...], jnp.zeros((6, width), F32)], axis=0)
    par[...] = padded(own_rows, 128)
    par[2:3] = padded(bias_up[...], 128)
    own_columns = par[...].T
    bias_a_column = own_columns[:width, 0:1]
    bias_b_column = own_columns[:width, 1:2]
    bias_up_column = own_columns[: width // 2, 2:3]
    stem_left = stem_left[:, :depth]

    remote(lat.at[both], lat.at[mates], lat_send.at[7], lat_recv.at[7], mate).wait_recv()
    depth = GROUPS * own_lat.shape[0]
    place = lax.broadcasted_iota(jnp.int32, (depth, depth), 0)
    taken = lax.broadcasted_iota(jnp.int32, (depth, depth), 1)
    quarter = depth // 4
    small = quarter // GROUPS
    source = lax.rem(place, quarter) // small * quarter + place // quarter * small + lax.rem(place, small)
    sorter = jnp.where(source == taken, 1.0, 0.0).astype(BF16)
    wide = jnp.concatenate(
        [dot(sorter, jnp.concatenate([lat[number, d] for number in order], axis=0)) for d in range(5)], axis=1
    )
    cell = start - 2 * span + lax.broadcasted_iota(jnp.int32, (1, 5 * span), 1)
    wide = jnp.where((cell >= 0) & (cell < total), wide, 0.0)
    views = {}
    for row in range(5):
        for tap in range(3):
            begin = 2 * span + (row - 2) * W + tap - 2
            view = padded(wide[:, begin : begin + span + 2])
            if tap == 0:
                view = jnp.where(inner_column == 0, 0.0, view)
            if tap == 2:
                view = jnp.where(inner_column == W - 1, 0.0, view)
            views[row, tap] = view.astype(BF16)

    def activate(values, gain_column, step):
        values = values.astype(F32)
        scale = lax.rsqrt(jnp.sum(values * values, axis=0, keepdims=True) * (1.0 / C) + EPS)
        values = values * scale * gain_column
        values = values / (1.0 + jnp.exp(-values))
        return jnp.where(inside(step), values, 0.0).astype(BF16)

    for frame in range(2):
        for step in range(3):
            right_side = jnp.concatenate(
                [
                    views[step + b, c][frame * quarter : (frame + 3) * quarter]
                    for b in range(3)
                    for c in range(3)
                ],
                axis=0,
            )
            values = (dot(stem_left, right_side) + bias_in_column).astype(BF16)
            if step == 1:
                stem[frame] = values.reshape(GROUPS, C // GROUPS, LANES)
            maps[2 + frame, step] = activate(values, gain_a_column, step)

    def windows(own, rim, frame):
        low, high = (jnp.concatenate([rim[number, side] for number in order], axis=0) for side in (LOW, HIGH))
        middle = jnp.concatenate([own[number, frame] for number in order], axis=0)
        return row_windows(frame, low, middle, high, span)

    def load_windows(own, rim):
        for frame in range(2):
            for step, values in enumerate(windows(own, rim, frame)):
                maps[frame, step] = jnp.where(inside(step), values, jnp.zeros_like(values))

    def taps(weight, frame, time_taps):
        first, count = time_taps[0], len(time_taps)
        rows = jnp.concatenate([weight[first * 3 + step] for step in range(3 * count)], axis=1)
        return dot(rows, maps[frame + first : frame + first + count].reshape(3 * count * C, LANES))

    def finish(acc, frame, bias_column, added):
        middle = acc[width : 2 * width]
        if added is not None:
            middle = middle + added.astype(F32)
        result = jnp.where(first_column, 0.0, acc[:width])
        result = result + pltpu.roll(middle, LANES - 1, 1)
        result = result + jnp.where(last_column, 0.0, pltpu.roll(acc[2 * width :], LANES - 2, 1))
        return (result + bias_column).astype(BF16)[:, :span]

    local[0].wait()
    early[0] = taps(wa, 0, (2,))
    early[1] = taps(wa, 1, (1, 2))
    take_mate(0, held_a, held_a_rim)
    load_windows(held_a, held_a_rim)
    for frame in range(2):
        acc = early[frame] + taps(wa, frame, (0, 1) if frame == 0 else (0,))
        swap_a[here, frame] = finish(acc, frame, bias_a_column, None)
    pack(2, swap_a)
    send_own(2, swap_a, swap_a_rim)

    pass_on(1, held_b, held_b_rim)
    take_mate(1, held_b, held_b_rim)
    load_windows(held_b, held_b_rim)
    local[1].wait()
    early[0] = taps(wb, 0, (0, 1))
    early[1] = taps(wb, 1, (0,))

    pass_on(2, swap_a, swap_a_rim)
    take_mate(2, swap_a, swap_a_rim)
    for frame in range(2):
        for step, values in enumerate(windows(swap_a, swap_a_rim, frame)):
            maps[2 + frame, step] = activate(values, gain_b_column, step)
    for frame in range(2):
        acc = early[frame] + taps(wb, frame, (2,) if frame == 0 else (1, 2))
        swap_b[here, frame] = finish(acc, frame, bias_b_column, stem[frame, chan])
    pack(3, swap_b)
    send_own(3, swap_b, swap_b_rim)

    local[2].wait()
    outs = C // GROUPS // 2
    row_sets = (((0,), (1, 2)), ((0, 1), (2,)))
    column_sets = ((0,), (1, 2), (0, 1), (2,))
    for p in range(2):
        for half in range(2):
            for block in range(4):
                summed = None
                for b in row_sets[p][half]:
                    for c in column_sets[block]:
                        term = wu[b * 3 + c].astype(F32)
                        summed = term if summed is None else summed + term
                up_left[p, block * outs : (block + 1) * outs, half * C : (half + 1) * C] = summed.astype(
                    BF16
                )
    half_lanes = LANES // 2
    into = lax.broadcasted_iota(jnp.int32, (4 * half_lanes, 4 * half_lanes), 1)
    whence = lax.broadcasted_iota(jnp.int32, (4 * half_lanes, 4 * half_lanes), 0)
    wanted = lax.rem(whence, half_lanes) * 4 + whence // half_lanes
    spread[...] = jnp.where(into == wanted, 1.0, 0.0).astype(BF16)

    pass_on(3, swap_b, swap_b_rim)
    take_mate(3, swap_b, swap_b_rim)
    load_windows(swap_b, swap_b_rim)
    pieces = []
    for frame in range(2):
        quarters = []
        for p in range(2):
            acc = dot(up_left[p], maps[frame, p : p + 2].reshape(2 * C, LANES))
            even = jnp.where(first_column, 0.0, acc[:outs]) + pltpu.roll(acc[outs : 2 * outs], LANES - 1, 1)
            odd = pltpu.roll(acc[2 * outs : 3 * outs], LANES - 1, 1) + jnp.where(
                last_column, 0.0, pltpu.roll(acc[3 * outs :], LANES - 2, 1)
            )
            quarters += [(even + bias_up_column).astype(BF16), (odd + bias_up_column).astype(BF16)]
        pieces.append(quarters)
    for frame in range(2):
        quarters = pieces[frame]
        for side in range(2):
            joined = jnp.concatenate(
                [part[:, side * half_lanes : (side + 1) * half_lanes] for part in quarters], axis=1
            )
            woven = dot(joined, spread[...]).astype(BF16)
            first = side * 4 * half_lanes
            count = min(4 * half_lanes, 4 * span - first)
            out[frame, :, first : first + count] = woven[:, :count]

    for condition, copy in sends:
        guarded(condition, copy.wait_send)


def shards(tiles, *operands):
    (
        latent,
        latent_cache,
        weight_in,
        bias_in,
        cache_a,
        gain_a,
        weight_a,
        bias_a,
        cache_b,
        gain_b,
        weight_b,
        bias_b,
        weight_up,
        bias_up,
    ) = operands
    span = latent.shape[2]
    width = C // GROUPS
    small = latent.shape[1]
    depth = 27 * weight_in.shape[4]
    vmem = pl.BlockSpec(memory_space=pltpu.VMEM)
    hbm = pl.BlockSpec(memory_space=pl.ANY)
    block = pltpu.VMEM((GROUPS, 2, width, span), BF16)
    rim = pltpu.VMEM((GROUPS, 2, width, 384), BF16)
    dma = pltpu.SemaphoreType.DMA
    row = lambda vector: vector.reshape(1, -1)
    return pl.pallas_call(
        functools.partial(body, tiles, span),
        out_shape=jax.ShapeDtypeStruct((2, width // 2, 4 * span), BF16),
        in_specs=[hbm] * 14,
        out_specs=vmem,
        scratch_shapes=[
            pltpu.VMEM(latent.shape, BF16),
            pltpu.VMEM(latent.shape, BF16),
            pltpu.VMEM((27, weight_in.shape[4], width), BF16),
            *[pltpu.VMEM((1, width), F32)] * 5,
            pltpu.VMEM((1, width // 2), F32),
            pltpu.VMEM((4 * small, span), BF16),
            pltpu.VMEM((GROUPS, 5, 4 * small, span), BF16),
            pltpu.VMEM((GROUPS, width, depth + 16), BF16),
            pltpu.VMEM((8, 128), F32),
            block,
            rim,
            block,
            rim,
            block,
            rim,
            block,
            rim,
            pltpu.VMEM((4, 2, width, 384), BF16),
            pltpu.VMEM((2, GROUPS, width, LANES), BF16),
            pltpu.VMEM((4, 3, C, LANES), BF16),
            pltpu.VMEM((2, 3 * width, LANES), F32),
            pltpu.VMEM((9, 3 * width, C), BF16),
            pltpu.VMEM((9, 3 * width, C), BF16),
            pltpu.VMEM((9, width // 2, C), BF16),
            pltpu.VMEM((2, 4 * width // 2, 2 * C), BF16),
            pltpu.VMEM((2 * LANES, 2 * LANES), BF16),
            dma((14,)),
            dma((8,)),
            dma((8,)),
            dma((2,)),
            dma((2,)),
            dma((4, 9)),
            dma((4, 9)),
        ],
        compiler_params=pltpu.CompilerParams(
            collective_id=0, has_side_effects=True, vmem_limit_bytes=48 << 20
        ),
    )(
        *(pltpu.with_memory_space_constraint(operand, pltpu.HBM) for operand in (
        latent,
        latent_cache,
        weight_in.swapaxes(3, 4).reshape(27, -1, width),
        row(bias_in),
        cache_a,
        row(gain_a),
        weight_a.reshape(9, 3 * width, C),
        row(bias_a),
        cache_b,
        row(gain_b),
        weight_b.reshape(9, 3 * width, C),
        row(bias_b),
        weight_up.reshape(9, width // 2, C),
        row(bias_up),
    )))


def solution(mesh):
    placed = (
        P(None, "chan", "tile"),
        P(None, "chan", "tile"),
        P(None, None, None, "chan", None),
        P("chan"),
        P(None, "chan", "tile"),
        P("chan"),
        P(None, None, None, "chan", None),
        P("chan"),
        P(None, "chan", "tile"),
        P("chan"),
        P(None, None, None, "chan", None),
        P("chan"),
        P(None, None, "chan", None),
        P("chan"),
    )
    return jax.shard_map(
        functools.partial(shards, mesh.shape["tile"]),
        mesh=mesh,
        in_specs=placed,
        out_specs=P(None, "chan", "tile"),
        check_vma=False,
    )
```
